32 devices in a mesh: plane: 2 (over x), coil: 16 (over z, y, core).
Axes of the slice: x: 2, y: 2, z: 4, core: 2. Of those that a mesh axis runs over, the one named last changes fastest.
Arguments:
- image: float32 [512, 8, 512], P(('plane', 'coil')), parts along dimension 0, may hold values from -6 to 6
- sens: float32 [512, 32, 512], P(('plane', 'coil')), parts along dimension 0, may hold values from -0.75 to 0.75
- kspace: float32 [512, 256, 512], P('plane', 'coil'), parts along dimension 0, may hold values from -6 to 6
- mask: int32 [8, 256], replicated, may hold values 0 or 1
Outputs:
- recon: float32 [512, 8, 512], P(('plane', 'coil')), parts along dimension 0
The draws below stay inside these ranges and needn't reach their ends.
There are 2 independent parts, one for each index of `plane`. The reference program is written for one: setup_inputs(seed, part) draws one part's arguments, and reference() takes and returns one part's arrays. A program takes and returns all parts, laid end to end along the dimension named above; an argument that names none is the same for every part. Nothing has to cross between parts.
Inputs may be any that keep to these rules, and one draw needn't show every extreme that they name: mask[f, ky] is 1 where phase-encode line ky is sampled in frame f, else 0.
All inputs are finite; a program needn't handle non-finite values.
Results may differ from the reference program's by a relative error of at most 0.0001.
Values sent between devices are 32-bit elements; how exact they have to be, the bound alone decides.
A program may use at most 128 MiB of HBM per device.

```python
import jax
import jax.numpy as jnp
from jax import lax

NY = 256
NZ = 256
COILS = 32
FRAMES = 8
OUTER = 2
INNER = 2


def plant(array, rng, least, top_value):
    spot = [jax.random.randint(jax.random.fold_in(rng, axis), (), 0, length) for axis, length in enumerate(array.shape)]
    longest = array.shape.index(max(array.shape))
    neighbour = spot[:longest] + [(spot[longest] + 1) % array.shape[longest]] + spot[longest + 1:]
    return array.at[tuple(spot)].set(least).at[tuple(neighbour)].set(top_value)


def steps_of(rng, extent, shards, low, top_value):
    level, own = 1.0, jax.random.fold_in(rng, 6)
    for axis_at, parts in shards:
        steps = jnp.exp(jax.random.uniform(jax.random.fold_in(own, axis_at), (parts,), jnp.float32, low / len(shards), top_value / len(shards)))
        level = level * jnp.repeat(steps, extent[axis_at] // parts).reshape([-1 if axis == axis_at else 1 for axis in range(len(extent))])
    return level


def centred(rng, dims, width, limit, cuts=(), held_as=jnp.bfloat16):
    level = steps_of(rng, dims, cuts, -0.22, 0.18) if cuts else 1.0
    values = jax.random.normal(rng, dims, jnp.float32) * width * level
    return jnp.minimum(jnp.maximum(values, -limit), limit).astype(held_as)


def setup_inputs(seed: int = 0, part: int = 0) -> dict:
    splits = jax.random.split(jax.random.key(seed), 5)
    part_splits = jax.random.split(jax.random.fold_in(splits[4], part), 5)
    return {
        "image": centred(part_splits[0], (NY, FRAMES, 2 * NZ), 1.0, 6.0, ((0, 16),), jnp.float32),
        "sens": centred(part_splits[1], (NY, COILS, 2 * NZ), 0.125, 0.75, ((0, 16),), jnp.float32),
        "kspace": centred(part_splits[2], (NY, COILS * FRAMES, 2 * NZ), 1.0, 6.0, ((1, 16),), jnp.float32),
        "mask": plant((jax.random.randint(splits[3], (FRAMES, NY), 0, 3) < 1).astype(jnp.int32), jax.random.fold_in(splits[3], 1), 0, 1),
    }


step_size = 0.5
tv_weight = 0.1
dual_step = 1.25


def unpack_complex(packed):
    half = packed.shape[-1] // 2
    return lax.complex(packed[..., :half], packed[..., half:])


def pack_complex(values):
    return jnp.concatenate([jnp.real(values), jnp.imag(values)], -1)


def forward_diff(field):
    diff_rows = jnp.concatenate([field[1:] - field[:-1], jnp.zeros_like(field[:1])], 0)
    diff_time = jnp.concatenate([field[:, 1:] - field[:, :-1], jnp.zeros_like(field[:, :1])], 1)
    return diff_time, diff_rows


def adjoint_diff(dual_time, dual_rows):
    keep_time = (lax.iota(jnp.int32, dual_time.shape[1]) < dual_time.shape[1] - 1)[None, :, None]
    keep_rows = (lax.iota(jnp.int32, dual_rows.shape[0]) < dual_rows.shape[0] - 1)[:, None, None]
    from_time = jnp.concatenate([jnp.zeros_like(dual_time[:, :1]), dual_time[:, :-1]], 1) - jnp.where(keep_time, dual_time, 0.0)
    from_rows = jnp.concatenate([jnp.zeros_like(dual_rows[:1]), dual_rows[:-1]], 0) - jnp.where(keep_rows, dual_rows, 0.0)
    return from_time + from_rows


def reference(image, sens, kspace, mask):
    maps = jnp.transpose(unpack_complex(sens), (1, 0, 2))
    data = jnp.transpose(unpack_complex(kspace).reshape(NY, COILS, FRAMES, NZ), (1, 2, 0, 3))
    sampled = mask.astype(jnp.float32)[:, :, None]
    field = image
    for sweep in range(OUTER):
        frames_now = jnp.transpose(unpack_complex(field), (1, 0, 2))

        def add_coil(total, coil_input):
            coil_map, coil_data = coil_input
            spectrum = jnp.fft.fft2(coil_map[None] * frames_now, axes=(1, 2), norm="ortho")
            residual = sampled * (spectrum - coil_data)
            term = jnp.conj(coil_map)[None] * jnp.fft.ifft2(residual, axes=(1, 2), norm="ortho")
            return total + term, None

        total, unused = lax.scan(add_coil, jnp.zeros_like(frames_now), (maps, data))
        gradient = pack_complex(jnp.transpose(total, (1, 0, 2)))
        target = field - step_size * gradient
        dual_time = jnp.zeros_like(target)
        dual_rows = jnp.zeros_like(target)
        for repeat in range(INNER):
            primal = target - tv_weight * adjoint_diff(dual_time, dual_rows)
            diff_time, diff_rows = forward_diff(primal)
            dual_time = jnp.clip(dual_time + dual_step * diff_time, -1.0, 1.0)
            dual_rows = jnp.clip(dual_rows + dual_step * diff_rows, -1.0, 1.0)
        field = target - tv_weight * adjoint_diff(dual_time, dual_rows)
    return field
```

```python
import jax
import jax.numpy as jnp
import numpy as np
from jax import lax
from jax.experimental import pallas as pl
from jax.experimental.pallas import tpu as pltpu
from jax.sharding import PartitionSpec as P

OUTER = 2
INNER = 2

step_size = 0.5
tv_weight = 0.1
dual_step = 1.25
high = lax.Precision.HIGH


def contract(spec, *operands):
    return jnp.einsum(spec, *operands, precision=high, preferred_element_type=jnp.float32)


def dft_tables(length):
    index = lax.iota(jnp.int32, length)
    product = index[:, None] * index[None, :] % length
    angle = 2.0 * jnp.pi / length * product.astype(jnp.float32)
    scale = 1.0 / jnp.sqrt(jnp.float32(length))
    return (jnp.cos(angle) * scale, -jnp.sin(angle) * scale)


def column_matrix(cos_part, sin_part):
    upper = jnp.concatenate([cos_part, sin_part], 1)
    lower = jnp.concatenate([-sin_part, cos_part], 1)
    return jnp.concatenate([upper, lower], 0)


def projections(mask, row_cos, row_sin):
    weights = mask.astype(jnp.float32)
    wide = jnp.concatenate([row_cos, row_sin], 1)
    cos_rows = weights[:, :, None] * row_cos[None]
    sin_rows = weights[:, :, None] * row_sin[None]
    from_cos = contract("fka,ky->fay", cos_rows, wide)
    from_sin = contract("fka,ky->fay", sin_rows, wide)
    length = row_cos.shape[0]
    real = from_cos[..., :length] + from_sin[..., length:]
    imag = from_cos[..., length:] - from_sin[..., :length]
    return (real, imag)


def to_columns(field, devices):
    rows, count, packed = field.shape
    width = packed // 2 // devices
    parts = field.reshape(rows, count, 2, devices, width)
    return jnp.transpose(parts, (3, 0, 2, 1, 4)).reshape(devices, rows, 2 * count * width)


def divergence(dual_time, dual_rows):
    time_axis, row_axis = 1, 3
    zero_time = jnp.zeros_like(dual_time[:, :1])
    zero_rows = jnp.zeros_like(dual_rows[..., :1])
    head_time = dual_time[:, :-1]
    head_rows = dual_rows[..., :-1]
    from_time = jnp.concatenate([zero_time, head_time], time_axis) - jnp.concatenate(
        [head_time, zero_time], time_axis
    )
    from_rows = jnp.concatenate([zero_rows, head_rows], row_axis) - jnp.concatenate(
        [head_rows, zero_rows], row_axis
    )
    return from_time + from_rows


def forward_diff(field):
    diff_time = jnp.concatenate(
        [field[:, 1:] - field[:, :-1], jnp.zeros_like(field[:, :1])], 1
    )
    diff_rows = jnp.concatenate(
        [field[..., 1:] - field[..., :-1], jnp.zeros_like(field[..., :1])], 3
    )
    return (diff_time, diff_rows)


def denoise(target):
    dual_time = jnp.zeros_like(target)
    dual_rows = jnp.zeros_like(target)
    for repeat in range(INNER):
        primal = target
        if repeat:
            primal = target - tv_weight * divergence(dual_time, dual_rows)
        diff_time, diff_rows = forward_diff(primal)
        dual_time = jnp.clip(dual_time + dual_step * diff_time, -1.0, 1.0)
        dual_rows = jnp.clip(dual_rows + dual_step * diff_rows, -1.0, 1.0)
    return target - tv_weight * divergence(dual_time, dual_rows)


def iterate(field, data_term, maps, real, imag):
    maps_re, maps_im = (maps[0][None], maps[1][None])
    for sweep in range(OUTER):
        now_re, now_im = (field[0][:, None], field[1][:, None])
        seen_re = maps_re * now_re - maps_im * now_im
        seen_im = maps_re * now_im + maps_im * now_re
        kept_re = contract("fczy,fky->fczk", seen_re, real) - contract(
            "fczy,fky->fczk", seen_im, imag
        )
        kept_im = contract("fczy,fky->fczk", seen_re, imag) + contract(
            "fczy,fky->fczk", seen_im, real
        )
        grad_re = jnp.sum(maps_re * kept_re + maps_im * kept_im, 1)
        grad_im = jnp.sum(maps_re * kept_im - maps_im * kept_re, 1)
        gradient = jnp.stack([grad_re, grad_im]) - data_term
        field = denoise(field - step_size * gradient)
    return field


def data_images(kspace, mask_pairs, row_cos, row_sin, col_cos, col_sin):
    masked = jnp.transpose(mask_pairs)[:, :, None] * kspace
    mid = contract("kpz,zw->kpw", masked, column_matrix(col_cos, -col_sin))
    half = kspace.shape[-1] // 2
    from_cos = contract("ky,kpz->ypz", row_cos, mid)
    from_sin = contract("ky,kpz->ypz", row_sin, mid)
    real = from_cos[..., :half] + from_sin[..., half:]
    imag = from_cos[..., half:] - from_sin[..., :half]
    return (real, imag)


LANES = 128
SUBLANES = 8


def swap_blocks(values, width):
    count = len(values)
    block = lax.broadcasted_iota(jnp.int32, values[0].shape, 1) // width
    step = count // 2
    while step:
        lower = block // step % 2 == 0
        shift = step * width
        values = list(values)
        for at in range(count):
            if at // step % 2 == 0:
                near, far = (values[at], values[at + step])
                values[at] = jnp.where(lower, near, pltpu.roll(far, shift, 1))
                values[at + step] = jnp.where(lower, pltpu.roll(near, LANES - shift, 1), far)
        step //= 2
    return values


def blocked(devices, width, rows, length, half, coils, frames, pairs):
    group = LANES // width
    fits = LANES % width == 0 and width % SUBLANES == 0 and rows % SUBLANES == 0
    fits = fits and devices % group == 0 and coils % group == 0 and frames % group == 0
    fits = fits and devices >= SUBLANES and devices & (devices - 1) == 0
    fits = fits and pairs % frames == 0 and coils * frames == pairs * devices
    return fits and length % (2 * LANES) == 0 and half % LANES == 0


def pack_kernel(devices, width, sens_ref, image_ref, out_ref):
    group = LANES // width
    half = devices * width
    start = 0
    for source in (sens_ref, image_ref):
        count = source.shape[0]
        for part in range(2):
            for tile in range(half // LANES):
                lane = part * half + tile * LANES
                for first in range(0, count, group):
                    taken = [source[first + at, :, lane : lane + LANES] for at in range(group)]
                    target = start + (part * count + first) * width
                    for at, value in enumerate(swap_blocks(taken, width)):
                        out_ref[tile * group + at, :, target : target + LANES] = value
        start += 2 * count * width


def split(value):
    top = value.astype(jnp.bfloat16)
    return (top, (value - top.astype(jnp.float32)).astype(jnp.bfloat16))


def narrow(value):
    value = value.astype(np.float32)
    top = value.astype(jnp.bfloat16)
    return np.stack([top, (value - top.astype(np.float32)).astype(jnp.bfloat16)])


def mix_left(value):
    top, low = split(value)
    return jnp.concatenate([low, top, top], 1)


def mix_right(pair):
    return jnp.concatenate([pair[0], pair[1], pair[0]], 0)


def dot(left, right):
    return jnp.dot(left, right, preferred_element_type=jnp.float32)


def row_tables(length):
    half = length // 2
    tables = []
    for odd in range(2):
        product = np.outer(np.arange(half), 2 * np.arange(half) + odd) % length
        angle = 2.0 * np.pi / length * product
        cos_part, sin_part = (np.cos(angle) / np.sqrt(length), np.sin(angle) / np.sqrt(length))
        tables.append(narrow(np.block([[cos_part, -sin_part], [sin_part, cos_part]])))
    return np.stack(tables)


def column_table(length):
    angle = 2.0 * np.pi / length * (np.outer(np.arange(length), np.arange(length)) % length)
    cos_part, sin_part = (np.cos(angle) / np.sqrt(length), np.sin(angle) / np.sqrt(length))
    return narrow(np.block([[cos_part, sin_part], [-sin_part, cos_part]]))


MESH = pl.DeviceIdType.MESH


def greet(peers):
    barrier = pltpu.get_barrier_semaphore()
    for peer in peers:
        pl.semaphore_signal(barrier, 1, device_id={"coil": peer}, device_id_type=MESH)
    pl.semaphore_wait(barrier, len(peers))


def shift_rows(value, step):
    length = value.shape[1]
    rolled = pltpu.roll(value, step % length, 1)
    at = lax.broadcasted_iota(jnp.int32, value.shape, 1)
    kept = at >= step if step > 0 else at < length + step
    return jnp.where(kept, rolled, 0.0)


def spread_rows(dual):
    return shift_rows(dual, 1) - dual


def row_steps(primal):
    length = primal.shape[1]
    at = lax.broadcasted_iota(jnp.int32, primal.shape, 1)
    return jnp.where(at < length - 1, pltpu.roll(primal, length - 1, 1) - primal, 0.0)


def clipped(value):
    return jnp.minimum(jnp.maximum(value, -1.0), 1.0)


def denoise_frames(target):
    frames = len(target)
    dual_time = [None] * frames
    dual_rows = [None] * frames

    def lowered(frame):
        moved = spread_rows(dual_rows[frame])
        if frame > 0:
            moved = moved + dual_time[frame - 1]
        if frame < frames - 1:
            moved = moved - dual_time[frame]
        return target[frame] - tv_weight * moved

    primal = target
    for repeat in range(INNER):
        if repeat:
            primal = [lowered(frame) for frame in range(frames)]
        for frame in range(frames):
            rows = dual_step * row_steps(primal[frame])
            dual_rows[frame] = clipped(rows if not repeat else dual_rows[frame] + rows)
            if frame < frames - 1:
                time = dual_step * (primal[frame + 1] - primal[frame])
                dual_time[frame] = clipped(time if not repeat else dual_time[frame] + time)
    return [lowered(frame) for frame in range(frames)]


def whole_kernel(
    devices,
    image_ref,
    sens_ref,
    kspace_ref,
    mask_ref,
    rows_ref,
    cols_ref,
    out_ref,
    sens_v,
    image_v,
    rows_v,
    cols_v,
    data_ref,
    mask_v,
    base_ref,
    maps_ref,
    packed_ref,
    landed_ref,
    own_ref,
    now_ref,
    grad_ref,
    gram_ref,
    ready_ref,
    back_ref,
    *rest,
):
    bits = devices.bit_length() - 1
    sums = rest[: bits + 1]
    gots = rest[bits + 1 : 2 * bits + 1]
    (
        load_sem,
        data_sem,
        maps_send,
        maps_recv,
        pack_send,
        pack_recv,
        sum_send,
        sum_recv,
        back_send,
        back_recv,
    ) = rest[2 * bits + 1 :]
    coils, frames, length, packed = base_ref.shape
    rows, all_coils, unused = sens_ref.shape
    half = packed // 2
    low = length // 2
    width = half // devices
    group = LANES // width
    me = lax.axis_index("coil")
    peers = [(me + hop) % devices for hop in range(1, devices)]
    own_bits = [me // (1 << bit) % 2 for bit in range(bits)]
    own_rows = pl.ds(pl.multiple_of(me * rows, SUBLANES), rows)

    loads = []

    def load(source, target):
        loads.append(pltpu.make_async_copy(source, target, load_sem.at[len(loads)]))
        loads[-1].start()

    for coil in range(all_coils):
        load(sens_ref.at[:, coil, :], sens_v.at[coil])
    for frame in range(frames):
        load(image_ref.at[:, frame, :], image_v.at[frame])
    load(rows_ref, rows_v)
    load(cols_ref, cols_v)

    def data_copy(pair, odd):
        return pltpu.make_async_copy(
            kspace_ref.at[:, odd, pair, :], data_ref.at[pair, odd], data_sem.at[pair, odd]
        )

    for pair in range(coils * frames):
        for odd in range(2):
            data_copy(pair, odd).start()

    def remote(source, target, send, recv, peer):
        return pltpu.make_async_remote_copy(
            src_ref=source,
            dst_ref=target,
            send_sem=send,
            recv_sem=recv,
            device_id={"coil": peer},
            device_id_type=MESH,
        )

    def maps_copy(hop, coil):
        peer = peers[hop - 1]
        return remote(
            sens_ref.at[:, peer * coils + coil, :],
            maps_ref.at[coil, own_rows, :],
            maps_send.at[hop - 1, coil],
            maps_recv.at[hop - 1, coil],
            peer,
        )

    def pack_copy(hop):
        peer = peers[hop - 1]
        return remote(
            packed_ref.at[peer],
            landed_ref.at[me],
            pack_send.at[hop - 1],
            pack_recv.at[hop - 1],
            peer,
        )

    def kept_part(stage, frame, other):
        at = own_bits[stage]
        at = 1 - at if other else at
        lead = (slice(None),) * (bits - 1 - stage)
        return sums[stage].at[(frame,) + lead + (at,)]

    def sum_copy(stage, frame):
        return remote(
            kept_part(stage, frame, True),
            gots[stage].at[frame],
            sum_send.at[frame, stage],
            sum_recv.at[frame, stage],
            me + (1 - 2 * own_bits[stage]) * (1 << stage),
        )

    def collect(stage, frame):
        sum_copy(stage, frame).wait_recv()
        sums[stage + 1][frame] = kept_part(stage, frame, False)[...] + gots[stage][frame]

    greet(peers)
    for hop in range(1, devices):
        for coil in range(coils):
            maps_copy(hop, coil).start()
    for copy in loads:
        copy.wait()
    pack_kernel(devices, width, sens_v, image_v, packed_ref)
    for hop in range(1, devices):
        pack_copy(hop).start()
    for coil in range(coils):
        maps_ref[coil, own_rows, :] = sens_v[me * coils + coil]
    landed_ref[me] = packed_ref[me]

    lane = lax.broadcasted_iota(jnp.int32, (length, 2 * length), 1)
    line = lax.broadcasted_iota(jnp.int32, (length, 2 * length), 0)
    picked = line == 2 * (lane % low) + lane // length
    mask_v[...] = dot(
        mask_ref[...].astype(jnp.float32).astype(jnp.bfloat16),
        jnp.where(picked, 1.0, 0.0).astype(jnp.bfloat16),
    )
    for pair in range(coils * frames):
        for odd in range(2):
            data_copy(pair, odd).wait()

    def transform(frame, unused):
        mixes = []
        for odd in range(2):
            weight = mask_v[pl.ds(frame, 1), odd * length : (odd + 1) * length].astype(jnp.bfloat16)
            top, rest_part = (rows_v[odd, 0] * weight, rows_v[odd, 1] * weight)
            mixes.append(jnp.concatenate([rest_part, top, top], 1))
            right = jnp.concatenate([rows_v[odd, 0], rows_v[odd, 1], rows_v[odd, 0]], 1)
            gram = lax.dot_general(
                mixes[-1], right, (((1,), (1,)), ((), ())), preferred_element_type=jnp.float32
            )
            top, rest_part = split(gram)
            gram_ref[frame, odd, 0] = top
            gram_ref[frame, odd, 1] = rest_part
        for coil in range(coils):
            parts = []
            for odd in range(2):
                lines = data_ref[coil * frames + frame, odd]
                lines = jnp.concatenate([lines[:, :half], lines[:, half:]], 0)
                parts.append(dot(mixes[odd], mix_right(split(lines))))
            near, far = (parts[0] + parts[1], parts[0] - parts[1])
            mid = jnp.concatenate(
                [
                    jnp.concatenate([near[:low], near[low:]], 1),
                    jnp.concatenate([far[:low], far[low:]], 1),
                ],
                0,
            )
            base_ref[coil, frame] = dot(mix_left(mid), mix_right(cols_v))
        return unused

    lax.fori_loop(0, frames, transform, 0)
    for hop in range(1, devices):
        for coil in range(coils):
            maps_copy(hop, coil).wait_recv()

    def weigh(frame):
        real, imag = (0.0, 0.0)
        for coil in range(coils):
            base_re, base_im = (base_ref[coil, frame, :, :half], base_ref[coil, frame, :, half:])
            maps_re, maps_im = (maps_ref[coil, :, :half], maps_ref[coil, :, half:])
            real = real + maps_re * base_re + maps_im * base_im
            imag = imag + maps_re * base_im - maps_im * base_re
        shape = (2,) * bits + (width, length)
        lead = (frame,) + (slice(None),) * bits
        sums[0][lead + (slice(0, width),)] = jnp.transpose(real).reshape(shape)
        sums[0][lead + (slice(width, 2 * width),)] = jnp.transpose(imag).reshape(shape)

    def project(frame):
        shape = (all_coils, width, length)
        maps_re, maps_im = (own_ref[0], own_ref[1])
        now_re, now_im = (now_ref[0, frame][None], now_ref[1, frame][None])
        seen_re = (maps_re * now_re - maps_im * now_im).reshape(all_coils * width, length)
        seen_im = (maps_re * now_im + maps_im * now_re).reshape(all_coils * width, length)
        parts = []
        for odd in range(2):
            if odd:
                both = [part[:, :low] - part[:, low:] for part in (seen_re, seen_im)]
            else:
                both = [part[:, :low] + part[:, low:] for part in (seen_re, seen_im)]
            parts.append(dot(mix_left(jnp.concatenate(both, 1)), mix_right(gram_ref[frame, odd])))
        near, far = (parts[0] + parts[1], parts[0] - parts[1])
        kept_re = jnp.concatenate([near[:, :low], far[:, :low]], 1).reshape(shape)
        kept_im = jnp.concatenate([near[:, low:], far[:, low:]], 1).reshape(shape)
        grad_ref[0, frame] = jnp.sum(maps_re * kept_re + maps_im * kept_im, 0)
        grad_ref[1, frame] = jnp.sum(maps_re * kept_im - maps_im * kept_re, 0)

    for turn in range(frames + 2):
        if turn < frames:
            weigh(turn)
            sum_copy(0, turn).start()
        for stage in range(2):
            frame = turn - 1 - stage
            if 0 <= frame < frames:
                collect(stage, frame)
                sum_copy(stage + 1, frame).start()

    for hop in range(1, devices):
        pack_copy(hop).wait_recv()
    cut = 2 * all_coils * width
    turned = jnp.transpose(landed_ref[...].reshape(length, landed_ref.shape[2]))
    own_ref[...] = turned[:cut].reshape(own_ref.shape)
    now_ref[...] = turned[cut:].reshape(now_ref.shape)
    for frame in range(frames):
        project(frame)
        collect(2, frame)
        for stage in range(3, bits):
            sum_copy(stage, frame).start()
            if stage < bits - 1:
                collect(stage, frame)
    for frame in range(frames):
        collect(bits - 1, frame)

    for sweep in range(OUTER):
        if sweep:
            for frame in range(frames):
                project(frame)
        for part in range(2):
            target = []
            for frame in range(frames):
                data_term = sums[bits][frame, part * width : (part + 1) * width]
                gradient = grad_ref[part, frame] - data_term
                target.append(now_ref[part, frame] - step_size * gradient)
            for frame, value in enumerate(denoise_frames(target)):
                now_ref[part, frame] = value

    turned = jnp.transpose(now_ref[...].reshape(2 * frames * width, length))
    ready_ref[...] = turned.reshape(ready_ref.shape)

    def back_copy(hop):
        peer = peers[hop - 1]
        return remote(
            ready_ref.at[peer], back_ref.at[me], back_send.at[hop - 1], back_recv.at[hop - 1], peer
        )

    for hop in range(1, devices):
        back_copy(hop).start()
    back_ref[me] = ready_ref[me]
    for hop in range(1, devices):
        back_copy(hop).wait_recv()
    for part in range(2):
        for first in range(0, frames, group):
            lane = (part * frames + first) * width
            for tile in range(devices // group):
                taken = [
                    back_ref[tile * group + at, :, lane : lane + LANES] for at in range(group)
                ]
                target = part * half + tile * LANES
                for at, value in enumerate(swap_blocks(taken, width)):
                    out_ref[:, first + at, target : target + LANES] = value
    for hop in range(1, devices):
        for coil in range(coils):
            maps_copy(hop, coil).wait_send()
        pack_copy(hop).wait_send()
        back_copy(hop).wait_send()
    for frame in range(frames):
        for stage in range(bits):
            sum_copy(stage, frame).wait_send()


def reconstruct(image, sens, kspace, mask, devices):
    rows, frames, packed = image.shape
    all_coils = sens.shape[1]
    length, pairs, unused = kspace.shape
    coils = pairs // frames
    bits = devices.bit_length() - 1
    width = packed // 2 // devices
    lanes = 2 * (all_coils + frames) * width
    row_pairs = row_tables(length)
    col_pair = column_table(packed // 2)
    whole = pl.BlockSpec(memory_space=pltpu.VMEM)
    apart = pl.BlockSpec(memory_space=pl.ANY)

    def held(*shape):
        return pltpu.VMEM(shape, jnp.float32)

    dma = pltpu.SemaphoreType.DMA
    block = (2 * width, length)
    sums = [held(frames, *(2,) * (bits - stage), *block) for stage in range(bits + 1)]
    gots = [held(frames, *(2,) * (bits - 1 - stage), *block) for stage in range(bits)]
    return pl.pallas_call(
        lambda *refs: whole_kernel(devices, *refs),
        out_shape=jax.ShapeDtypeStruct((rows, frames, packed), jnp.float32),
        in_specs=[apart] * 3 + [whole] + [apart] * 2,
        out_specs=whole,
        scratch_shapes=[
            held(all_coils, rows, packed),
            held(frames, rows, packed),
            pltpu.VMEM(row_pairs.shape, jnp.bfloat16),
            pltpu.VMEM(col_pair.shape, jnp.bfloat16),
            held(pairs, 2, length // 2, packed),
            held(frames, 2 * length),
            held(coils, frames, length, packed),
            held(coils, length, packed),
            held(devices, rows, lanes),
            held(devices, rows, lanes),
            held(2, all_coils, width, length),
            held(2, frames, width, length),
            held(2, frames, width, length),
            pltpu.VMEM((frames, 2, 2, length, length), jnp.bfloat16),
            held(devices, rows, 2 * frames * width),
            held(devices, rows, 2 * frames * width),
            *sums,
            *gots,
            dma((all_coils + frames + 2,)),
            dma((pairs, 2)),
            dma((devices - 1, coils)),
            dma((devices - 1, coils)),
            dma((devices - 1,)),
            dma((devices - 1,)),
            dma((frames, bits)),
            dma((frames, bits)),
            dma((devices - 1,)),
            dma((devices - 1,)),
        ],
        compiler_params=pltpu.CompilerParams(
            collective_id=0, has_side_effects=True, vmem_limit_bytes=60 * 1024 * 1024
        ),
        name="reconstruct",
    )(
        image,
        sens,
        kspace.reshape(length // 2, 2, pairs, packed),
        mask,
        jnp.asarray(row_pairs),
        jnp.asarray(col_pair),
    )


def per_device(image, sens, kspace, mask):
    devices = lax.axis_size("coil")
    device = lax.axis_index("coil")
    rows_dev, frames, packed = image.shape
    coils = sens.shape[1]
    length, pairs, unused = kspace.shape
    half = packed // 2
    width = half // devices
    copies = max(1, frames // pairs)
    own_coils = max(1, pairs // frames)
    own_frames = min(frames, pairs)
    if blocked(devices, width, rows_dev, length, half, coils, frames, pairs):
        return reconstruct(image, sens, kspace, mask, devices)
    row_cos, row_sin = dft_tables(length)
    col_cos, col_sin = dft_tables(half)
    mask_float = mask.astype(jnp.float32)
    real, imag = projections(mask, row_cos, row_sin)
    spread = sens if copies == 1 else jnp.repeat(sens, copies, axis=1)
    own_maps = lax.all_to_all(spread, "coil", split_axis=1, concat_axis=0, tiled=True)
    outgoing = jnp.concatenate([to_columns(sens, devices), to_columns(image, devices)], 2)
    incoming = lax.all_to_all(outgoing, "coil", split_axis=0, concat_axis=0, tiled=True)
    columns = jnp.transpose(incoming.reshape(length, -1))
    first_frame = device * pairs % frames
    local_mask = lax.dynamic_slice_in_dim(mask_float, first_frame, own_frames, 0)
    mask_pairs = jnp.tile(local_mask, (own_coils, 1))
    base_re, base_im = data_images(kspace, mask_pairs, row_cos, row_sin, col_cos, col_sin)
    base_re = base_re.reshape(length, own_coils, own_frames, half)
    base_im = base_im.reshape(length, own_coils, own_frames, half)
    own_re, own_im = (own_maps[:, :, None, :half], own_maps[:, :, None, half:])
    term_re = jnp.sum(own_re * base_re + own_im * base_im, 1)
    term_im = jnp.sum(own_re * base_im - own_im * base_re, 1)
    term = jnp.transpose(jnp.stack([term_re, term_im]), (3, 0, 2, 1))
    if own_frames < frames:
        wide = jnp.zeros((half, 2, frames, length), jnp.float32)
        term = lax.dynamic_update_slice_in_dim(wide, term, first_frame, 2)
    term = term.reshape(devices, width, 2, frames, length)
    data_term = lax.psum_scatter(term, "coil", scatter_dimension=0, tiled=True)
    data_term = jnp.transpose(data_term[0], (1, 2, 0, 3))

    cut = 2 * coils * width
    maps = columns[:cut].reshape(2, coils, width, length)
    field = columns[cut:].reshape(2, frames, width, length)
    field = iterate(field, data_term, maps, real, imag)

    leaving = jnp.transpose(field.reshape(2 * frames * width, length))
    leaving = leaving.reshape(devices, rows_dev, 2 * frames * width)
    arrived = lax.all_to_all(leaving, "coil", split_axis=0, concat_axis=0, tiled=True)
    arrived = arrived.reshape(devices, rows_dev, 2, frames, width)
    return jnp.transpose(arrived, (1, 3, 2, 0, 4)).reshape(rows_dev, frames, packed)


def solution(mesh):
    return jax.shard_map(
        per_device,
        mesh=mesh,
        in_specs=(
            P(("plane", "coil"), None, None),
            P(("plane", "coil"), None, None),
            P("plane", "coil", None),
            P(),
        ),
        out_specs=P(("plane", "coil"), None, None),
        check_vma=False,
    )
```

```python
import jax
import jax.numpy as jnp
import numpy as np
from jax import lax
from jax.experimental import pallas as pl
from jax.experimental.pallas import tpu as pltpu
from jax.sharding import PartitionSpec as P

OUTER = 2
INNER = 2

step_size = 0.5
tv_weight = 0.1
dual_step = 1.25
high = lax.Precision.HIGH


def contract(spec, *operands):
    return jnp.einsum(spec, *operands, precision=high, preferred_element_type=jnp.float32)


def dft_tables(length):
    index = lax.iota(jnp.int32, length)
    product = index[:, None] * index[None, :] % length
    angle = 2.0 * jnp.pi / length * product.astype(jnp.float32)
    scale = 1.0 / jnp.sqrt(jnp.float32(length))
    return (jnp.cos(angle) * scale, -jnp.sin(angle) * scale)


def column_matrix(cos_part, sin_part):
    upper = jnp.concatenate([cos_part, sin_part], 1)
    lower = jnp.concatenate([-sin_part, cos_part], 1)
    return jnp.concatenate([upper, lower], 0)


def projections(mask, row_cos, row_sin):
    weights = mask.astype(jnp.float32)
    wide = jnp.concatenate([row_cos, row_sin], 1)
    cos_rows = weights[:, :, None] * row_cos[None]
    sin_rows = weights[:, :, None] * row_sin[None]
    from_cos = contract("fka,ky->fay", cos_rows, wide)
    from_sin = contract("fka,ky->fay", sin_rows, wide)
    length = row_cos.shape[0]
    real = from_cos[..., :length] + from_sin[..., length:]
    imag = from_cos[..., length:] - from_sin[..., :length]
    return (real, imag)


def to_columns(field, devices):
    rows, count, packed = field.shape
    width = packed // 2 // devices
    parts = field.reshape(rows, count, 2, devices, width)
    return jnp.transpose(parts, (3, 0, 2, 1, 4)).reshape(devices, rows, 2 * count * width)


def divergence(dual_time, dual_rows):
    time_axis, row_axis = 1, 3
    zero_time = jnp.zeros_like(dual_time[:, :1])
    zero_rows = jnp.zeros_like(dual_rows[..., :1])
    head_time = dual_time[:, :-1]
    head_rows = dual_rows[..., :-1]
    from_time = jnp.concatenate([zero_time, head_time], time_axis) - jnp.concatenate(
        [head_time, zero_time], time_axis
    )
    from_rows = jnp.concatenate([zero_rows, head_rows], row_axis) - jnp.concatenate(
        [head_rows, zero_rows], row_axis
    )
    return from_time + from_rows


def forward_diff(field):
    diff_time = jnp.concatenate(
        [field[:, 1:] - field[:, :-1], jnp.zeros_like(field[:, :1])], 1
    )
    diff_rows = jnp.concatenate(
        [field[..., 1:] - field[..., :-1], jnp.zeros_like(field[..., :1])], 3
    )
    return (diff_time, diff_rows)


def denoise(target):
    dual_time = jnp.zeros_like(target)
    dual_rows = jnp.zeros_like(target)
    for repeat in range(INNER):
        primal = target
        if repeat:
            primal = target - tv_weight * divergence(dual_time, dual_rows)
        diff_time, diff_rows = forward_diff(primal)
        dual_time = jnp.clip(dual_time + dual_step * diff_time, -1.0, 1.0)
        dual_rows = jnp.clip(dual_rows + dual_step * diff_rows, -1.0, 1.0)
    return target - tv_weight * divergence(dual_time, dual_rows)


def iterate(field, data_term, maps, real, imag):
    maps_re, maps_im = (maps[0][None], maps[1][None])
    for sweep in range(OUTER):
        now_re, now_im = (field[0][:, None], field[1][:, None])
        seen_re = maps_re * now_re - maps_im * now_im
        seen_im = maps_re * now_im + maps_im * now_re
        kept_re = contract("fczy,fky->fczk", seen_re, real) - contract(
            "fczy,fky->fczk", seen_im, imag
        )
        kept_im = contract("fczy,fky->fczk", seen_re, imag) + contract(
            "fczy,fky->fczk", seen_im, real
        )
        grad_re = jnp.sum(maps_re * kept_re + maps_im * kept_im, 1)
        grad_im = jnp.sum(maps_re * kept_im - maps_im * kept_re, 1)
        gradient = jnp.stack([grad_re, grad_im]) - data_term
        field = denoise(field - step_size * gradient)
    return field


def data_images(kspace, mask_pairs, row_cos, row_sin, col_cos, col_sin):
    masked = jnp.transpose(mask_pairs)[:, :, None] * kspace
    mid = contract("kpz,zw->kpw", masked, column_matrix(col_cos, -col_sin))
    half = kspace.shape[-1] // 2
    from_cos = contract("ky,kpz->ypz", row_cos, mid)
    from_sin = contract("ky,kpz->ypz", row_sin, mid)
    real = from_cos[..., :half] + from_sin[..., half:]
    imag = from_cos[..., half:] - from_sin[..., :half]
    return (real, imag)


LANES = 128
SUBLANES = 8


def swap_blocks(values, width):
    count = len(values)
    block = lax.broadcasted_iota(jnp.int32, values[0].shape, 1) // width
    step = count // 2
    while step:
        lower = block // step % 2 == 0
        shift = step * width
        values = list(values)
        for at in range(count):
            if at // step % 2 == 0:
                near, far = (values[at], values[at + step])
                values[at] = jnp.where(lower, near, pltpu.roll(far, shift, 1))
                values[at + step] = jnp.where(lower, pltpu.roll(near, LANES - shift, 1), far)
        step //= 2
    return values


def blocked(devices, width, rows, length, half, coils, frames, pairs):
    group = LANES // width
    fits = LANES % width == 0 and width % SUBLANES == 0 and rows % SUBLANES == 0
    fits = fits and devices % group == 0 and coils % (2 * group) == 0 and frames % group == 0
    fits = fits and devices & (devices - 1) == 0
    fits = fits and devices >= 16 and pairs % frames == 0 and coils * frames == pairs * devices
    return fits and length % (2 * LANES) == 0 and half % (2 * LANES) == 0


def pack_kernel(devices, width, sens_ref, image_ref, out_ref):
    group = LANES // width
    half = devices * width
    near = sens_ref.shape[0] // 2
    start = 0
    for source, origin, count in (
        (sens_ref, 0, near),
        (image_ref, 0, image_ref.shape[0]),
        (sens_ref, near, near),
    ):
        for part in range(2):
            for tile in range(half // LANES):
                lane = part * half + tile * LANES
                for first in range(0, count, group):
                    taken = [
                        source[origin + first + at, :, lane : lane + LANES] for at in range(group)
                    ]
                    target = start + (part * count + first) * width
                    for at, value in enumerate(swap_blocks(taken, width)):
                        out_ref[tile * group + at, :, target : target + LANES] = value
        start += 2 * count * width


def split(value):
    top = value.astype(jnp.bfloat16)
    return (top, (value - top.astype(jnp.float32)).astype(jnp.bfloat16))


def narrow(value):
    value = value.astype(np.float32)
    top = value.astype(jnp.bfloat16)
    return np.stack([top, (value - top.astype(np.float32)).astype(jnp.bfloat16)])


def mix_left(value):
    top, low = split(value)
    return jnp.concatenate([low, top, top], 1)


def mix_right(pair):
    return jnp.concatenate([pair[0], pair[1], pair[0]], 0)


def dot(left, right):
    return jnp.dot(left, right, preferred_element_type=jnp.float32)


def row_tables(length):
    half = length // 2
    tables = []
    for odd in range(2):
        product = np.outer(np.arange(half), 2 * np.arange(half) + odd) % length
        angle = 2.0 * np.pi / length * product
        cos_part, sin_part = (np.cos(angle) / np.sqrt(length), np.sin(angle) / np.sqrt(length))
        tables.append(narrow(np.block([[cos_part, -sin_part], [sin_part, cos_part]])))
    return np.stack(tables)


def column_table(length):
    angle = 2.0 * np.pi / length * (np.outer(np.arange(length), np.arange(length)) % length)
    cos_part, sin_part = (np.cos(angle) / np.sqrt(length), np.sin(angle) / np.sqrt(length))
    return narrow(np.block([[cos_part, sin_part], [-sin_part, cos_part]]))


MESH = pl.DeviceIdType.MESH


def greet(peers):
    barrier = pltpu.get_barrier_semaphore()
    for peer in peers:
        pl.semaphore_signal(barrier, 1, device_id={"coil": peer}, device_id_type=MESH)
    pl.semaphore_wait(barrier, len(peers))


def shift_rows(value, step):
    length = value.shape[1]
    rolled = pltpu.roll(value, step % length, 1)
    at = lax.broadcasted_iota(jnp.int32, value.shape, 1)
    kept = at >= step if step > 0 else at < length + step
    return jnp.where(kept, rolled, 0.0)


def spread_rows(dual):
    return shift_rows(dual, 1) - dual


def row_steps(primal):
    length = primal.shape[1]
    at = lax.broadcasted_iota(jnp.int32, primal.shape, 1)
    return jnp.where(at < length - 1, pltpu.roll(primal, length - 1, 1) - primal, 0.0)


def clipped(value):
    return jnp.minimum(jnp.maximum(value, -1.0), 1.0)


def denoise_frames(target):
    frames = len(target)
    dual_time = [None] * frames
    dual_rows = [None] * frames

    def lowered(frame):
        moved = spread_rows(dual_rows[frame])
        if frame > 0:
            moved = moved + dual_time[frame - 1]
        if frame < frames - 1:
            moved = moved - dual_time[frame]
        return target[frame] - tv_weight * moved

    primal = target
    for repeat in range(INNER):
        if repeat:
            primal = [lowered(frame) for frame in range(frames)]
        for frame in range(frames):
            rows = dual_step * row_steps(primal[frame])
            dual_rows[frame] = clipped(rows if not repeat else dual_rows[frame] + rows)
            if frame < frames - 1:
                time = dual_step * (primal[frame + 1] - primal[frame])
                dual_time[frame] = clipped(time if not repeat else dual_time[frame] + time)
    return [lowered(frame) for frame in range(frames)]


def whole_kernel(
    devices,
    image_ref,
    sens_ref,
    kspace_ref,
    mask_ref,
    rows_ref,
    cols_ref,
    out_ref,
    sens_v,
    image_v,
    rows_v,
    cols_v,
    data_ref,
    mask_v,
    base_ref,
    maps_ref,
    packed_ref,
    landed_ref,
    own_ref,
    now_ref,
    grad_ref,
    gram_ref,
    relay_ref,
    ready_ref,
    back_ref,
    *rest,
):
    bits = devices.bit_length() - 1
    sums = rest[: bits + 1]
    gots = rest[bits + 1 : 2 * bits + 1]
    (
        load_sem,
        data_sem,
        maps_send,
        maps_recv,
        pack_send,
        pack_recv,
        relay_send,
        relay_recv,
        sum_send,
        sum_recv,
        back_send,
        back_recv,
    ) = rest[2 * bits + 1 :]
    coils, frames, length, packed = base_ref.shape
    rows, all_coils, unused = sens_ref.shape
    half = packed // 2
    low = length // 2
    width = half // devices
    group = LANES // width
    me = lax.axis_index("coil")
    own_bits = [me // (1 << bit) % 2 for bit in range(bits)]
    peers = []
    for hop in range(1, devices):
        flips = [(own_bits[bit] + (hop >> bit)) % 2 * (1 << bit) for bit in range(bits)]
        peers.append(sum(flips[1:], flips[0]))
    near = devices // 2
    side = me // near
    far_side = 1 - side
    near_hops = list(range(1, near))
    far_hops = list(range(near, devices))
    block = all_coils * width
    held_lanes = 2 * frames * width
    own_rows = pl.ds(pl.multiple_of(me * rows, SUBLANES), rows)

    loads = []

    def load(source, target):
        loads.append(pltpu.make_async_copy(source, target, load_sem.at[len(loads)]))
        loads[-1].start()

    for coil in range(all_coils):
        load(sens_ref.at[:, coil, :], sens_v.at[coil])
    for frame in range(frames):
        load(image_ref.at[:, frame, :], image_v.at[frame])
    load(rows_ref, rows_v)
    load(cols_ref, cols_v)

    def data_copy(pair, odd):
        return pltpu.make_async_copy(
            kspace_ref.at[:, odd, pair, :], data_ref.at[pair, odd], data_sem.at[pair, odd]
        )

    for pair in range(coils * frames):
        for odd in range(2):
            data_copy(pair, odd).start()

    def remote(source, target, send, recv, peer):
        return pltpu.make_async_remote_copy(
            src_ref=source,
            dst_ref=target,
            send_sem=send,
            recv_sem=recv,
            device_id={"coil": peer},
            device_id_type=MESH,
        )

    def maps_copy(hop, coil):
        peer = peers[hop - 1]
        return remote(
            sens_ref.at[:, peer * coils + coil, :],
            maps_ref.at[coil, own_rows, :],
            maps_send.at[hop - 1, coil],
            maps_recv.at[hop - 1, coil],
            peer,
        )

    def pack_copy(hop):
        peer = peers[hop - 1]
        if hop < near:
            lanes = pl.ds(0, 2 * block + held_lanes)
        else:
            lanes = pl.ds(pl.multiple_of(side * block, LANES), block + held_lanes)
        return remote(
            packed_ref.at[peer, :, lanes],
            landed_ref.at[me, :, lanes],
            pack_send.at[hop - 1],
            pack_recv.at[hop - 1],
            peer,
        )

    def relay_part(coil_side, first, row_side):
        lanes = pl.ds(pl.multiple_of(row_side * low, LANES), low)
        return own_ref.at[coil_side, :, pl.ds(first, coils), :, lanes]

    def relay_copy(hop):
        peer = peers[hop - 1]
        return remote(
            relay_ref.at[peer % near],
            relay_part(side, me % near * coils, far_side),
            relay_send.at[hop - 1],
            relay_recv.at[hop - 1],
            peer,
        )

    def kept_part(stage, frame, other):
        at = own_bits[stage]
        at = 1 - at if other else at
        lead = (slice(None),) * (bits - 1 - stage)
        return sums[stage].at[(frame,) + lead + (at,)]

    def sum_copy(stage, frame):
        return remote(
            kept_part(stage, frame, True),
            gots[stage].at[frame],
            sum_send.at[frame, stage],
            sum_recv.at[frame, stage],
            me + (1 - 2 * own_bits[stage]) * (1 << stage),
        )

    def collect(stage, frame):
        sum_copy(stage, frame).wait_recv()
        sums[stage + 1][frame] = kept_part(stage, frame, False)[...] + gots[stage][frame]

    greet(peers)
    early = near // 2
    for far_hop, near_hop in zip(far_hops[:early], near_hops[:early]):
        for hop in (far_hop, near_hop):
            for coil in range(coils):
                maps_copy(hop, coil).start()
    for copy in loads:
        copy.wait()
    pack_kernel(devices, width, sens_v, image_v, packed_ref)
    for at in range(near):
        if at < early:
            for coil in range(coils):
                maps_copy(far_hops[early + at], coil).start()
        if early <= at < near - 1:
            for coil in range(coils):
                maps_copy(near_hops[at], coil).start()
        if at < near - 1:
            pack_copy(near_hops[at]).start()
    for hop in far_hops:
        pack_copy(hop).start()
    for coil in range(coils):
        maps_ref[coil, own_rows, :] = sens_v[me * coils + coil]
    landed_ref[me] = packed_ref[me]

    lane = lax.broadcasted_iota(jnp.int32, (length, 2 * length), 1)
    line = lax.broadcasted_iota(jnp.int32, (length, 2 * length), 0)
    picked = line == 2 * (lane % low) + lane // length
    mask_v[...] = dot(
        mask_ref[...].astype(jnp.float32).astype(jnp.bfloat16),
        jnp.where(picked, 1.0, 0.0).astype(jnp.bfloat16),
    )
    for pair in range(coils * frames):
        for odd in range(2):
            data_copy(pair, odd).wait()

    def transform(frame, unused):
        mixes = []
        for odd in range(2):
            weight = mask_v[pl.ds(frame, 1), odd * length : (odd + 1) * length].astype(jnp.bfloat16)
            top, rest_part = (rows_v[odd, 0] * weight, rows_v[odd, 1] * weight)
            mixes.append(jnp.concatenate([rest_part, top, top], 1))
            right = jnp.concatenate([rows_v[odd, 0], rows_v[odd, 1], rows_v[odd, 0]], 1)
            gram = lax.dot_general(
                mixes[-1], right, (((1,), (1,)), ((), ())), preferred_element_type=jnp.float32
            )
            top, rest_part = split(gram)
            gram_ref[frame, odd, 0] = top
            gram_ref[frame, odd, 1] = rest_part
        for coil in range(coils):
            parts = []
            for odd in range(2):
                lines = data_ref[coil * frames + frame, odd]
                lines = jnp.concatenate([lines[:, :half], lines[:, half:]], 0)
                parts.append(dot(mixes[odd], mix_right(split(lines))))
            near, far = (parts[0] + parts[1], parts[0] - parts[1])
            mid = jnp.concatenate(
                [
                    jnp.concatenate([near[:low], near[low:]], 1),
                    jnp.concatenate([far[:low], far[low:]], 1),
                ],
                0,
            )
            base_ref[coil, frame] = dot(mix_left(mid), mix_right(cols_v))
        return unused

    lax.fori_loop(0, frames, transform, 0)
    for hop in range(1, devices):
        for coil in range(coils):
            maps_copy(hop, coil).wait_recv()

    def weigh(frame):
        real, imag = (0.0, 0.0)
        for coil in range(coils):
            base_re, base_im = (base_ref[coil, frame, :, :half], base_ref[coil, frame, :, half:])
            maps_re, maps_im = (maps_ref[coil, :, :half], maps_ref[coil, :, half:])
            real = real + maps_re * base_re + maps_im * base_im
            imag = imag + maps_re * base_im - maps_im * base_re
        shape = (2,) * bits + (width, length)
        lead = (frame,) + (slice(None),) * bits
        sums[0][lead + (slice(0, width),)] = jnp.transpose(real).reshape(shape)
        sums[0][lead + (slice(width, 2 * width),)] = jnp.transpose(imag).reshape(shape)

    def project(frame):
        shape = (all_coils, width, length)
        maps_re, maps_im = (own_ref[:, 0].reshape(shape), own_ref[:, 1].reshape(shape))
        now_re, now_im = (now_ref[0, frame][None], now_ref[1, frame][None])
        seen_re = (maps_re * now_re - maps_im * now_im).reshape(all_coils * width, length)
        seen_im = (maps_re * now_im + maps_im * now_re).reshape(all_coils * width, length)
        parts = []
        for odd in range(2):
            if odd:
                both = [part[:, :low] - part[:, low:] for part in (seen_re, seen_im)]
            else:
                both = [part[:, :low] + part[:, low:] for part in (seen_re, seen_im)]
            parts.append(dot(mix_left(jnp.concatenate(both, 1)), mix_right(gram_ref[frame, odd])))
        near, far = (parts[0] + parts[1], parts[0] - parts[1])
        kept_re = jnp.concatenate([near[:, :low], far[:, :low]], 1).reshape(shape)
        kept_im = jnp.concatenate([near[:, low:], far[:, low:]], 1).reshape(shape)
        grad_ref[0, frame] = jnp.sum(maps_re * kept_re + maps_im * kept_im, 0)
        grad_ref[1, frame] = jnp.sum(maps_re * kept_im - maps_im * kept_re, 0)

    def turn_maps():
        lines = pl.ds(pl.multiple_of(far_side * low, LANES), low)
        for coil in range(coils):
            for part in range(2):
                lanes = pl.ds(pl.multiple_of(part * half + side * (half // 2), LANES), half // 2)
                turned = jnp.transpose(maps_ref[coil, lines, lanes])
                relay_ref[:, part, coil] = turned.reshape(near, width, low)
        for hop in near_hops:
            relay_copy(hop).start()
        relay_part(side, me % near * coils, far_side)[...] = relay_ref[me % near]

    lags = [1, 2] + [2 + 2 * stage for stage in range(1, bits - 2)]
    for turn in range(frames + lags[-1]):
        if turn < frames:
            weigh(turn)
            sum_copy(0, turn).start()
        for stage, lag in enumerate(lags):
            if 0 <= turn - lag < frames:
                collect(stage, turn - lag)
                sum_copy(stage + 1, turn - lag).start()
        if turn == 0:
            turn_maps()

    for hop in range(1, devices):
        pack_copy(hop).wait_recv()
    for hop in near_hops:
        relay_copy(hop).wait_recv()

    def unfold(target, row_side, lines, lanes):
        turned = jnp.transpose(landed_ref[lines, :, lanes].reshape(low, -1))
        rows_at = pl.ds(pl.multiple_of(row_side * low, LANES), low)
        target[..., rows_at] = turned.reshape(target.shape[:-1] + (low,))

    for row_side in (side, far_side):
        lines = pl.ds(row_side * near, near)
        unfold(now_ref, row_side, lines, pl.ds(block, held_lanes))
    for coil_side, row_side in ((0, side), (1, side), (far_side, far_side)):
        start = pl.multiple_of(coil_side * (block + held_lanes), LANES)
        lines = pl.ds(row_side * near, near)
        unfold(own_ref.at[coil_side], row_side, lines, pl.ds(start, block))
    for frame in range(frames):
        project(frame)
        collect(bits - 1, frame)

    for sweep in range(OUTER):
        if sweep:
            for frame in range(frames):
                project(frame)
        for part in range(2):
            target = []
            for frame in range(frames):
                data_term = sums[bits][frame, part * width : (part + 1) * width]
                gradient = grad_ref[part, frame] - data_term
                target.append(now_ref[part, frame] - step_size * gradient)
            for frame, value in enumerate(denoise_frames(target)):
                now_ref[part, frame] = value

    turned = jnp.transpose(now_ref[...].reshape(2 * frames * width, length))
    ready_ref[...] = turned.reshape(ready_ref.shape)

    def back_copy(hop):
        peer = peers[hop - 1]
        return remote(
            ready_ref.at[peer], back_ref.at[me], back_send.at[hop - 1], back_recv.at[hop - 1], peer
        )

    for hop in range(1, devices):
        back_copy(hop).start()
    back_ref[me] = ready_ref[me]
    for hop in range(1, devices):
        back_copy(hop).wait_recv()
    for part in range(2):
        for first in range(0, frames, group):
            lane = (part * frames + first) * width
            for tile in range(devices // group):
                taken = [
                    back_ref[tile * group + at, :, lane : lane + LANES] for at in range(group)
                ]
                target = part * half + tile * LANES
                for at, value in enumerate(swap_blocks(taken, width)):
                    out_ref[:, first + at, target : target + LANES] = value
    for hop in range(1, devices):
        for coil in range(coils):
            maps_copy(hop, coil).wait_send()
        pack_copy(hop).wait_send()
        if hop < near:
            relay_copy(hop).wait_send()
        back_copy(hop).wait_send()
    for frame in range(frames):
        for stage in range(bits):
            sum_copy(stage, frame).wait_send()


def reconstruct(image, sens, kspace, mask, devices):
    rows, frames, packed = image.shape
    all_coils = sens.shape[1]
    length, pairs, unused = kspace.shape
    coils = pairs // frames
    bits = devices.bit_length() - 1
    width = packed // 2 // devices
    lanes = 2 * (all_coils + frames) * width
    row_pairs = row_tables(length)
    col_pair = column_table(packed // 2)
    whole = pl.BlockSpec(memory_space=pltpu.VMEM)
    apart = pl.BlockSpec(memory_space=pl.ANY)

    def held(*shape):
        return pltpu.VMEM(shape, jnp.float32)

    dma = pltpu.SemaphoreType.DMA
    block = (2 * width, length)
    sums = [held(frames, *(2,) * (bits - stage), *block) for stage in range(bits + 1)]
    gots = [held(frames, *(2,) * (bits - 1 - stage), *block) for stage in range(bits)]
    return pl.pallas_call(
        lambda *refs: whole_kernel(devices, *refs),
        out_shape=jax.ShapeDtypeStruct((rows, frames, packed), jnp.float32),
        in_specs=[apart] * 3 + [whole] + [apart] * 2,
        out_specs=whole,
        scratch_shapes=[
            held(all_coils, rows, packed),
            held(frames, rows, packed),
            pltpu.VMEM(row_pairs.shape, jnp.bfloat16),
            pltpu.VMEM(col_pair.shape, jnp.bfloat16),
            held(pairs, 2, length // 2, packed),
            held(frames, 2 * length),
            held(coils, frames, length, packed),
            held(coils, length, packed),
            held(devices, rows, lanes),
            held(devices, rows, lanes),
            held(2, 2, all_coils // 2, width, length),
            held(2, frames, width, length),
            held(2, frames, width, length),
            pltpu.VMEM((frames, 2, 2, length, length), jnp.bfloat16),
            held(devices // 2, 2, coils, width, length // 2),
            held(devices, rows, 2 * frames * width),
            held(devices, rows, 2 * frames * width),
            *sums,
            *gots,
            dma((all_coils + frames + 2,)),
            dma((pairs, 2)),
            dma((devices - 1, coils)),
            dma((devices - 1, coils)),
            dma((devices - 1,)),
            dma((devices - 1,)),
            dma((devices // 2 - 1,)),
            dma((devices // 2 - 1,)),
            dma((frames, bits)),
            dma((frames, bits)),
            dma((devices - 1,)),
            dma((devices - 1,)),
        ],
        compiler_params=pltpu.CompilerParams(
            collective_id=0, has_side_effects=True, vmem_limit_bytes=60 * 1024 * 1024
        ),
        name="reconstruct",
    )(
        image,
        sens,
        kspace.reshape(length // 2, 2, pairs, packed),
        mask,
        jnp.asarray(row_pairs),
        jnp.asarray(col_pair),
    )


def per_device(image, sens, kspace, mask):
    devices = lax.axis_size("coil")
    device = lax.axis_index("coil")
    rows_dev, frames, packed = image.shape
    coils = sens.shape[1]
    length, pairs, unused = kspace.shape
    half = packed // 2
    width = half // devices
    copies = max(1, frames // pairs)
    own_coils = max(1, pairs // frames)
    own_frames = min(frames, pairs)
    if blocked(devices, width, rows_dev, length, half, coils, frames, pairs):
        return reconstruct(image, sens, kspace, mask, devices)
    row_cos, row_sin = dft_tables(length)
    col_cos, col_sin = dft_tables(half)
    mask_float = mask.astype(jnp.float32)
    real, imag = projections(mask, row_cos, row_sin)
    spread = sens if copies == 1 else jnp.repeat(sens, copies, axis=1)
    own_maps = lax.all_to_all(spread, "coil", split_axis=1, concat_axis=0, tiled=True)
    outgoing = jnp.concatenate([to_columns(sens, devices), to_columns(image, devices)], 2)
    incoming = lax.all_to_all(outgoing, "coil", split_axis=0, concat_axis=0, tiled=True)
    columns = jnp.transpose(incoming.reshape(length, -1))
    first_frame = device * pairs % frames
    local_mask = lax.dynamic_slice_in_dim(mask_float, first_frame, own_frames, 0)
    mask_pairs = jnp.tile(local_mask, (own_coils, 1))
    base_re, base_im = data_images(kspace, mask_pairs, row_cos, row_sin, col_cos, col_sin)
    base_re = base_re.reshape(length, own_coils, own_frames, half)
    base_im = base_im.reshape(length, own_coils, own_frames, half)
    own_re, own_im = (own_maps[:, :, None, :half], own_maps[:, :, None, half:])
    term_re = jnp.sum(own_re * base_re + own_im * base_im, 1)
    term_im = jnp.sum(own_re * base_im - own_im * base_re, 1)
    term = jnp.transpose(jnp.stack([term_re, term_im]), (3, 0, 2, 1))
    if own_frames < frames:
        wide = jnp.zeros((half, 2, frames, length), jnp.float32)
        term = lax.dynamic_update_slice_in_dim(wide, term, first_frame, 2)
    term = term.reshape(devices, width, 2, frames, length)
    data_term = lax.psum_scatter(term, "coil", scatter_dimension=0, tiled=True)
    data_term = jnp.transpose(data_term[0], (1, 2, 0, 3))

    cut = 2 * coils * width
    maps = columns[:cut].reshape(2, coils, width, length)
    field = columns[cut:].reshape(2, frames, width, length)
    field = iterate(field, data_term, maps, real, imag)

    leaving = jnp.transpose(field.reshape(2 * frames * width, length))
    leaving = leaving.reshape(devices, rows_dev, 2 * frames * width)
    arrived = lax.all_to_all(leaving, "coil", split_axis=0, concat_axis=0, tiled=True)
    arrived = arrived.reshape(devices, rows_dev, 2, frames, width)
    return jnp.transpose(arrived, (1, 3, 2, 0, 4)).reshape(rows_dev, frames, packed)


def solution(mesh):
    return jax.shard_map(
        per_device,
        mesh=mesh,
        in_specs=(
            P(("plane", "coil"), None, None),
            P(("plane", "coil"), None, None),
            P("plane", "coil", None),
            P(),
        ),
        out_specs=P(("plane", "coil"), None, None),
        check_vma=False,
    )
```

```python
import jax
import jax.numpy as jnp
import numpy as np
from jax import lax
from jax.experimental import pallas as pl
from jax.experimental.pallas import tpu as pltpu
from jax.sharding import PartitionSpec as P

OUTER = 2
INNER = 2

step_size = 0.5
tv_weight = 0.1
dual_step = 1.25
high = lax.Precision.HIGH


def contract(spec, *operands):
    return jnp.einsum(spec, *operands, precision=high, preferred_element_type=jnp.float32)


def dft_tables(length):
    index = lax.iota(jnp.int32, length)
    product = index[:, None] * index[None, :] % length
    angle = 2.0 * jnp.pi / length * product.astype(jnp.float32)
    scale = 1.0 / jnp.sqrt(jnp.float32(length))
    return (jnp.cos(angle) * scale, -jnp.sin(angle) * scale)


def column_matrix(cos_part, sin_part):
    upper = jnp.concatenate([cos_part, sin_part], 1)
    lower = jnp.concatenate([-sin_part, cos_part], 1)
    return jnp.concatenate([upper, lower], 0)


def projections(mask, row_cos, row_sin):
    weights = mask.astype(jnp.float32)
    wide = jnp.concatenate([row_cos, row_sin], 1)
    cos_rows = weights[:, :, None] * row_cos[None]
    sin_rows = weights[:, :, None] * row_sin[None]
    from_cos = contract("fka,ky->fay", cos_rows, wide)
    from_sin = contract("fka,ky->fay", sin_rows, wide)
    length = row_cos.shape[0]
    real = from_cos[..., :length] + from_sin[..., length:]
    imag = from_cos[..., length:] - from_sin[..., :length]
    return (real, imag)


def to_columns(field, devices):
    rows, count, packed = field.shape
    width = packed // 2 // devices
    parts = field.reshape(rows, count, 2, devices, width)
    return jnp.transpose(parts, (3, 0, 2, 1, 4)).reshape(devices, rows, 2 * count * width)


def divergence(dual_time, dual_rows):
    time_axis, row_axis = 1, 3
    zero_time = jnp.zeros_like(dual_time[:, :1])
    zero_rows = jnp.zeros_like(dual_rows[..., :1])
    head_time = dual_time[:, :-1]
    head_rows = dual_rows[..., :-1]
    from_time = jnp.concatenate([zero_time, head_time], time_axis) - jnp.concatenate(
        [head_time, zero_time], time_axis
    )
    from_rows = jnp.concatenate([zero_rows, head_rows], row_axis) - jnp.concatenate(
        [head_rows, zero_rows], row_axis
    )
    return from_time + from_rows


def forward_diff(field):
    diff_time = jnp.concatenate(
        [field[:, 1:] - field[:, :-1], jnp.zeros_like(field[:, :1])], 1
    )
    diff_rows = jnp.concatenate(
        [field[..., 1:] - field[..., :-1], jnp.zeros_like(field[..., :1])], 3
    )
    return (diff_time, diff_rows)


def denoise(target):
    dual_time = jnp.zeros_like(target)
    dual_rows = jnp.zeros_like(target)
    for repeat in range(INNER):
        primal = target
        if repeat:
            primal = target - tv_weight * divergence(dual_time, dual_rows)
        diff_time, diff_rows = forward_diff(primal)
        dual_time = jnp.clip(dual_time + dual_step * diff_time, -1.0, 1.0)
        dual_rows = jnp.clip(dual_rows + dual_step * diff_rows, -1.0, 1.0)
    return target - tv_weight * divergence(dual_time, dual_rows)


def iterate(field, data_term, maps, real, imag):
    maps_re, maps_im = (maps[0][None], maps[1][None])
    for sweep in range(OUTER):
        now_re, now_im = (field[0][:, None], field[1][:, None])
        seen_re = maps_re * now_re - maps_im * now_im
        seen_im = maps_re * now_im + maps_im * now_re
        kept_re = contract("fczy,fky->fczk", seen_re, real) - contract(
            "fczy,fky->fczk", seen_im, imag
        )
        kept_im = contract("fczy,fky->fczk", seen_re, imag) + contract(
            "fczy,fky->fczk", seen_im, real
        )
        grad_re = jnp.sum(maps_re * kept_re + maps_im * kept_im, 1)
        grad_im = jnp.sum(maps_re * kept_im - maps_im * kept_re, 1)
        gradient = jnp.stack([grad_re, grad_im]) - data_term
        field = denoise(field - step_size * gradient)
    return field


def data_images(kspace, mask_pairs, row_cos, row_sin, col_cos, col_sin):
    masked = jnp.transpose(mask_pairs)[:, :, None] * kspace
    mid = contract("kpz,zw->kpw", masked, column_matrix(col_cos, -col_sin))
    half = kspace.shape[-1] // 2
    from_cos = contract("ky,kpz->ypz", row_cos, mid)
    from_sin = contract("ky,kpz->ypz", row_sin, mid)
    real = from_cos[..., :half] + from_sin[..., half:]
    imag = from_cos[..., half:] - from_sin[..., :half]
    return (real, imag)


LANES = 128
SUBLANES = 8


def swap_blocks(values, width):
    count = len(values)
    block = lax.broadcasted_iota(jnp.int32, values[0].shape, 1) // width
    step = count // 2
    while step:
        lower = block // step % 2 == 0
        shift = step * width
        values = list(values)
        for at in range(count):
            if at // step % 2 == 0:
                near, far = (values[at], values[at + step])
                values[at] = jnp.where(lower, near, pltpu.roll(far, shift, 1))
                values[at + step] = jnp.where(lower, pltpu.roll(near, LANES - shift, 1), far)
        step //= 2
    return values


def blocked(devices, width, rows, length, half, coils, frames, pairs):
    group = LANES // width
    fits = LANES % width == 0 and width % SUBLANES == 0 and rows % SUBLANES == 0
    fits = fits and devices % group == 0 and coils % (2 * group) == 0 and frames % group == 0
    fits = fits and devices & (devices - 1) == 0
    fits = fits and devices >= 16 and pairs % frames == 0 and coils * frames == pairs * devices
    return fits and length % (2 * LANES) == 0 and half % (2 * LANES) == 0


def pack_kernel(devices, width, sens_ref, image_ref, out_ref):
    group = LANES // width
    half = devices * width
    near = sens_ref.shape[0] // 2
    start = 0
    for source, origin, count in (
        (sens_ref, 0, near),
        (image_ref, 0, image_ref.shape[0]),
        (sens_ref, near, near),
    ):
        for part in range(2):
            for tile in range(half // LANES):
                lane = part * half + tile * LANES
                for first in range(0, count, group):
                    taken = [
                        source[origin + first + at, :, lane : lane + LANES] for at in range(group)
                    ]
                    target = start + (part * count + first) * width
                    for at, value in enumerate(swap_blocks(taken, width)):
                        out_ref[tile * group + at, :, target : target + LANES] = value
        start += 2 * count * width


def split(value):
    top = value.astype(jnp.bfloat16)
    return (top, (value - top.astype(jnp.float32)).astype(jnp.bfloat16))


def narrow(value):
    value = value.astype(np.float32)
    top = value.astype(jnp.bfloat16)
    return np.stack([top, (value - top.astype(np.float32)).astype(jnp.bfloat16)])


def mix_left(value):
    top, low = split(value)
    return jnp.concatenate([low, top, top], 1)


def mix_right(pair):
    return jnp.concatenate([pair[0], pair[1], pair[0]], 0)


def dot(left, right):
    return jnp.dot(left, right, preferred_element_type=jnp.float32)


def row_tables(length):
    half = length // 2
    tables = []
    for odd in range(2):
        product = np.outer(np.arange(half), 2 * np.arange(half) + odd) % length
        angle = 2.0 * np.pi / length * product
        cos_part, sin_part = (np.cos(angle) / np.sqrt(length), np.sin(angle) / np.sqrt(length))
        tables.append(narrow(np.block([[cos_part, -sin_part], [sin_part, cos_part]])))
    return np.stack(tables)


def column_table(length):
    angle = 2.0 * np.pi / length * (np.outer(np.arange(length), np.arange(length)) % length)
    cos_part, sin_part = (np.cos(angle) / np.sqrt(length), np.sin(angle) / np.sqrt(length))
    return narrow(np.block([[cos_part, sin_part], [-sin_part, cos_part]]))


MESH = pl.DeviceIdType.MESH


def greet(peers):
    barrier = pltpu.get_barrier_semaphore()
    for peer in peers:
        pl.semaphore_signal(barrier, 1, device_id={"coil": peer}, device_id_type=MESH)
    pl.semaphore_wait(barrier, len(peers))


def shift_rows(value, step):
    length = value.shape[1]
    rolled = pltpu.roll(value, step % length, 1)
    at = lax.broadcasted_iota(jnp.int32, value.shape, 1)
    kept = at >= step if step > 0 else at < length + step
    return jnp.where(kept, rolled, 0.0)


def spread_rows(dual):
    return shift_rows(dual, 1) - dual


def row_steps(primal):
    length = primal.shape[1]
    at = lax.broadcasted_iota(jnp.int32, primal.shape, 1)
    return jnp.where(at < length - 1, pltpu.roll(primal, length - 1, 1) - primal, 0.0)


def clipped(value):
    return jnp.minimum(jnp.maximum(value, -1.0), 1.0)


def denoise_frames(target):
    frames = len(target)
    dual_time = [None] * frames
    dual_rows = [None] * frames

    def lowered(frame):
        moved = spread_rows(dual_rows[frame])
        if frame > 0:
            moved = moved + dual_time[frame - 1]
        if frame < frames - 1:
            moved = moved - dual_time[frame]
        return target[frame] - tv_weight * moved

    primal = target
    for repeat in range(INNER):
        if repeat:
            primal = [lowered(frame) for frame in range(frames)]
        for frame in range(frames):
            rows = dual_step * row_steps(primal[frame])
            dual_rows[frame] = clipped(rows if not repeat else dual_rows[frame] + rows)
            if frame < frames - 1:
                time = dual_step * (primal[frame + 1] - primal[frame])
                dual_time[frame] = clipped(time if not repeat else dual_time[frame] + time)
    return [lowered(frame) for frame in range(frames)]


def whole_kernel(
    devices,
    image_ref,
    sens_ref,
    kspace_ref,
    mask_ref,
    rows_ref,
    cols_ref,
    out_ref,
    sens_v,
    image_v,
    rows_v,
    cols_v,
    data_ref,
    mask_v,
    base_ref,
    maps_ref,
    packed_ref,
    landed_ref,
    own_ref,
    now_ref,
    grad_ref,
    gram_ref,
    relay_ref,
    total_ref,
    ready_ref,
    back_ref,
    *rest,
):
    bits = devices.bit_length() - 1
    sums = rest[:bits]
    gots = rest[bits : 2 * bits]
    (
        load_sem,
        data_sem,
        maps_send,
        maps_recv,
        pack_send,
        pack_recv,
        relay_send,
        relay_recv,
        sum_send,
        sum_recv,
        back_send,
        back_recv,
    ) = rest[2 * bits :]
    coils, frames, length, packed = base_ref.shape
    rows, all_coils, unused = sens_ref.shape
    half = packed // 2
    low = length // 2
    width = half // devices
    group = LANES // width
    me = lax.axis_index("coil")
    own_bits = [me // (1 << bit) % 2 for bit in range(bits)]
    peers = []
    for hop in range(1, devices):
        flips = [(own_bits[bit] + (hop >> bit)) % 2 * (1 << bit) for bit in range(bits)]
        peers.append(sum(flips[1:], flips[0]))
    near = devices // 2
    side = me // near
    far_side = 1 - side
    near_hops = list(range(1, near))
    far_hops = list(range(near, devices))
    block = all_coils * width
    held_lanes = 2 * frames * width
    own_rows = pl.ds(pl.multiple_of(me * rows, SUBLANES), rows)

    loads = []

    def load(source, target):
        loads.append(pltpu.make_async_copy(source, target, load_sem.at[len(loads)]))
        loads[-1].start()

    for coil in range(all_coils):
        load(sens_ref.at[:, coil, :], sens_v.at[coil])
    for frame in range(frames):
        load(image_ref.at[:, frame, :], image_v.at[frame])
    load(rows_ref, rows_v)
    load(cols_ref, cols_v)

    def data_copy(pair, odd):
        return pltpu.make_async_copy(
            kspace_ref.at[:, odd, pair, :], data_ref.at[pair, odd], data_sem.at[pair, odd]
        )

    for pair in range(coils * frames):
        for odd in range(2):
            data_copy(pair, odd).start()

    def remote(source, target, send, recv, peer):
        return pltpu.make_async_remote_copy(
            src_ref=source,
            dst_ref=target,
            send_sem=send,
            recv_sem=recv,
            device_id={"coil": peer},
            device_id_type=MESH,
        )

    def maps_copy(hop, coil):
        peer = peers[hop - 1]
        return remote(
            sens_ref.at[:, peer * coils + coil, :],
            maps_ref.at[coil, own_rows, :],
            maps_send.at[hop - 1, coil],
            maps_recv.at[hop - 1, coil],
            peer,
        )

    def pack_copy(hop):
        peer = peers[hop - 1]
        if hop < near:
            lanes = pl.ds(0, 2 * block + held_lanes)
        else:
            lanes = pl.ds(pl.multiple_of(side * block, LANES), block + held_lanes)
        return remote(
            packed_ref.at[peer, :, lanes],
            landed_ref.at[me, :, lanes],
            pack_send.at[hop - 1],
            pack_recv.at[hop - 1],
            peer,
        )

    def relay_part(coil_side, first, row_side):
        lanes = pl.ds(pl.multiple_of(row_side * low, LANES), low)
        return own_ref.at[coil_side, :, pl.ds(first, coils), :, lanes]

    def relay_copy(hop):
        peer = peers[hop - 1]
        return remote(
            relay_ref.at[peer % near],
            relay_part(side, me % near * coils, far_side),
            relay_send.at[hop - 1],
            relay_recv.at[hop - 1],
            peer,
        )

    def kept_part(stage, phase, frame, other):
        at = own_bits[stage]
        at = 1 - at if other else at
        lead = (slice(None),) * (bits - 1 - stage)
        return sums[stage].at[(phase, frame) + lead + (at,)]

    def sum_copy(stage, phase, frame):
        landing = 1 - phase if stage == bits - 1 else phase
        return remote(
            kept_part(stage, phase, frame, True),
            gots[stage].at[landing, frame],
            sum_send.at[phase, frame, stage],
            sum_recv.at[landing, frame, stage],
            me + (1 - 2 * own_bits[stage]) * (1 << stage),
        )

    def side_rows(phase):
        row_side = far_side if phase else side
        return pl.ds(pl.multiple_of(row_side * low, LANES), low)

    def collect(stage, phase, frame):
        last = stage == bits - 1
        sum_copy(stage, 1 - phase if last else phase, frame).wait_recv()
        total = kept_part(stage, phase, frame, False)[...] + gots[stage][phase, frame]
        if last:
            total_ref[frame, :, side_rows(phase)] = total
        else:
            sums[stage + 1][phase, frame] = total

    greet(peers)
    early = near // 2
    for hop in near_hops + far_hops[:early]:
        for coil in range(coils):
            maps_copy(hop, coil).start()
    for copy in loads:
        copy.wait()
    pack_kernel(devices, width, sens_v, image_v, packed_ref)
    for at in range(near - 1):
        if at < early:
            for coil in range(coils):
                maps_copy(far_hops[early + at], coil).start()
        pack_copy(near_hops[at]).start()
    for hop in far_hops:
        if hop // 2 % 2 == 0:
            pack_copy(hop).start()
    for coil in range(coils):
        maps_ref[coil, own_rows, :] = sens_v[me * coils + coil]
    landed_ref[me] = packed_ref[me]

    lane = lax.broadcasted_iota(jnp.int32, (length, 2 * length), 1)
    line = lax.broadcasted_iota(jnp.int32, (length, 2 * length), 0)
    picked = line == 2 * (lane % low) + lane // length
    mask_v[...] = dot(
        mask_ref[...].astype(jnp.float32).astype(jnp.bfloat16),
        jnp.where(picked, 1.0, 0.0).astype(jnp.bfloat16),
    )
    for pair in range(coils * frames):
        for odd in range(2):
            data_copy(pair, odd).wait()

    def transform(frame):
        mixes = []
        for odd in range(2):
            weight = mask_v[pl.ds(frame, 1), odd * length : (odd + 1) * length].astype(jnp.bfloat16)
            top, rest_part = (rows_v[odd, 0] * weight, rows_v[odd, 1] * weight)
            mixes.append(jnp.concatenate([rest_part, top, top], 1))
            right = jnp.concatenate([rows_v[odd, 0], rows_v[odd, 1], rows_v[odd, 0]], 1)
            gram = lax.dot_general(
                mixes[-1], right, (((1,), (1,)), ((), ())), preferred_element_type=jnp.float32
            )
            top, rest_part = split(gram)
            gram_ref[frame, odd, 0] = top
            gram_ref[frame, odd, 1] = rest_part
        for coil in range(coils):
            parts = []
            for odd in range(2):
                lines = data_ref[coil * frames + frame, odd]
                lines = jnp.concatenate([lines[:, :half], lines[:, half:]], 0)
                parts.append(dot(mixes[odd], mix_right(split(lines))))
            near, far = (parts[0] + parts[1], parts[0] - parts[1])
            mid = jnp.concatenate(
                [
                    jnp.concatenate([near[:low], near[low:]], 1),
                    jnp.concatenate([far[:low], far[low:]], 1),
                ],
                0,
            )
            base_ref[coil, frame] = dot(mix_left(mid), mix_right(cols_v))

    def weigh(phase, frame):
        real, imag = (0.0, 0.0)
        lines = side_rows(phase)
        for coil in range(coils):
            base_re, base_im = (
                base_ref[coil, frame, lines, :half],
                base_ref[coil, frame, lines, half:],
            )
            maps_re, maps_im = (maps_ref[coil, lines, :half], maps_ref[coil, lines, half:])
            real = real + maps_re * base_re + maps_im * base_im
            imag = imag + maps_re * base_im - maps_im * base_re
        shape = (2,) * bits + (width, low)
        lead = (phase, frame) + (slice(None),) * bits
        sums[0][lead + (slice(0, width),)] = jnp.transpose(real).reshape(shape)
        sums[0][lead + (slice(width, 2 * width),)] = jnp.transpose(imag).reshape(shape)

    def pass_on(stage, phase, frame):
        if 0 <= frame < frames:
            collect(stage, phase, frame)
            sum_copy(stage + 1, phase, frame).start()

    def offer(phase, frame):
        if frame < frames:
            weigh(phase, frame)
            sum_copy(0, phase, frame).start()
        pass_on(0, phase, frame - 1)

    lead = min(3, frames - 1)

    def step(frame, unused):
        transform(frame)

        @pl.when(frame == lead)
        def wait_near():
            for hop in near_hops:
                for coil in range(coils):
                    maps_copy(hop, coil).wait_recv()

        @pl.when(frame >= lead)
        def offer_near():
            weigh(0, frame - lead)
            sum_copy(0, 0, frame - lead).start()

        @pl.when(frame > lead)
        def pass_near():
            collect(0, 0, frame - lead - 1)
            sum_copy(1, 0, frame - lead - 1).start()

        return unused

    lax.fori_loop(0, frames, step, 0)
    for turn in range(frames - lead, frames + 1):
        offer(0, turn)
    for hop in far_hops:
        if hop // 2 % 2:
            pack_copy(hop).start()
    for hop in far_hops:
        for coil in range(coils):
            maps_copy(hop, coil).wait_recv()

    def project(frame):
        shape = (all_coils, width, length)
        maps_re, maps_im = (own_ref[:, 0].reshape(shape), own_ref[:, 1].reshape(shape))
        now_re, now_im = (now_ref[0, frame][None], now_ref[1, frame][None])
        seen_re = (maps_re * now_re - maps_im * now_im).reshape(all_coils * width, length)
        seen_im = (maps_re * now_im + maps_im * now_re).reshape(all_coils * width, length)
        parts = []
        for odd in range(2):
            if odd:
                both = [part[:, :low] - part[:, low:] for part in (seen_re, seen_im)]
            else:
                both = [part[:, :low] + part[:, low:] for part in (seen_re, seen_im)]
            parts.append(dot(mix_left(jnp.concatenate(both, 1)), mix_right(gram_ref[frame, odd])))
        near, far = (parts[0] + parts[1], parts[0] - parts[1])
        kept_re = jnp.concatenate([near[:, :low], far[:, :low]], 1).reshape(shape)
        kept_im = jnp.concatenate([near[:, low:], far[:, low:]], 1).reshape(shape)
        grad_ref[0, frame] = jnp.sum(maps_re * kept_re + maps_im * kept_im, 0)
        grad_ref[1, frame] = jnp.sum(maps_re * kept_im - maps_im * kept_re, 0)

    def turn_maps():
        lines = pl.ds(pl.multiple_of(far_side * low, LANES), low)
        for coil in range(coils):
            for part in range(2):
                lanes = pl.ds(pl.multiple_of(part * half + side * (half // 2), LANES), half // 2)
                turned = jnp.transpose(maps_ref[coil, lines, lanes])
                relay_ref[:, part, coil] = turned.reshape(near, width, low)
        for hop in near_hops:
            relay_copy(hop).start()
        relay_part(side, me % near * coils, far_side)[...] = relay_ref[me % near]

    def unfold(target, row_side, lines, lanes):
        turned = jnp.transpose(landed_ref[lines, :, lanes].reshape(low, -1))
        rows_at = pl.ds(pl.multiple_of(row_side * low, LANES), low)
        target[..., rows_at] = turned.reshape(target.shape[:-1] + (low,))

    def take_columns():
        for hop in range(1, devices):
            pack_copy(hop).wait_recv()
        for hop in near_hops:
            relay_copy(hop).wait_recv()
        for row_side in (side, far_side):
            lines = pl.ds(row_side * near, near)
            unfold(now_ref, row_side, lines, pl.ds(block, held_lanes))
        for coil_side, row_side in ((0, side), (1, side), (far_side, far_side)):
            start = pl.multiple_of(coil_side * (block + held_lanes), LANES)
            lines = pl.ds(row_side * near, near)
            unfold(own_ref.at[coil_side], row_side, lines, pl.ds(start, block))

    for turn in range(frames + 1):
        offer(1, turn)
        if turn == 0:
            turn_maps()
        pass_on(1, 0, turn)
    for stage in range(2, bits - 2):
        for turn in range(frames):
            pass_on(stage - 1, 1, turn)
            pass_on(stage, 0, turn)
    first = min(1, frames - 1)
    for turn in range(frames + 2):
        if turn < frames:
            pass_on(bits - 3, 1, turn)
            pass_on(bits - 2, 0, turn)
        pass_on(bits - 2, 1, turn - 2)
        if turn == first:
            take_columns()
        if first <= turn < frames:
            project(turn - first)
    for frame in range(frames - first, frames):
        project(frame)
    for phase in range(2):
        for frame in range(frames):
            collect(bits - 1, phase, frame)

    for sweep in range(OUTER):
        if sweep:
            for frame in range(frames):
                project(frame)
        for part in range(2):
            target = []
            for frame in range(frames):
                data_term = total_ref[frame, part * width : (part + 1) * width]
                gradient = grad_ref[part, frame] - data_term
                target.append(now_ref[part, frame] - step_size * gradient)
            for frame, value in enumerate(denoise_frames(target)):
                now_ref[part, frame] = value

    turned = jnp.transpose(now_ref[...].reshape(2 * frames * width, length))
    ready_ref[...] = turned.reshape(ready_ref.shape)

    def back_copy(hop):
        peer = peers[hop - 1]
        return remote(
            ready_ref.at[peer], back_ref.at[me], back_send.at[hop - 1], back_recv.at[hop - 1], peer
        )

    for hop in range(1, devices):
        back_copy(hop).start()
    back_ref[me] = ready_ref[me]
    for hop in range(1, devices):
        back_copy(hop).wait_recv()
    for part in range(2):
        for first in range(0, frames, group):
            lane = (part * frames + first) * width
            for tile in range(devices // group):
                taken = [
                    back_ref[tile * group + at, :, lane : lane + LANES] for at in range(group)
                ]
                target = part * half + tile * LANES
                for at, value in enumerate(swap_blocks(taken, width)):
                    out_ref[:, first + at, target : target + LANES] = value
    for hop in range(1, devices):
        for coil in range(coils):
            maps_copy(hop, coil).wait_send()
        pack_copy(hop).wait_send()
        if hop < near:
            relay_copy(hop).wait_send()
        back_copy(hop).wait_send()
    for frame in range(frames):
        for stage in range(bits):
            for phase in range(2):
                sum_copy(stage, phase, frame).wait_send()


def reconstruct(image, sens, kspace, mask, devices):
    rows, frames, packed = image.shape
    all_coils = sens.shape[1]
    length, pairs, unused = kspace.shape
    coils = pairs // frames
    bits = devices.bit_length() - 1
    width = packed // 2 // devices
    lanes = 2 * (all_coils + frames) * width
    row_pairs = row_tables(length)
    col_pair = column_table(packed // 2)
    whole = pl.BlockSpec(memory_space=pltpu.VMEM)
    apart = pl.BlockSpec(memory_space=pl.ANY)

    def held(*shape):
        return pltpu.VMEM(shape, jnp.float32)

    dma = pltpu.SemaphoreType.DMA
    block = (2 * width, length // 2)
    sums = [held(2, frames, *(2,) * (bits - stage), *block) for stage in range(bits)]
    gots = [held(2, frames, *(2,) * (bits - 1 - stage), *block) for stage in range(bits)]
    return pl.pallas_call(
        lambda *refs: whole_kernel(devices, *refs),
        out_shape=jax.ShapeDtypeStruct((rows, frames, packed), jnp.float32),
        in_specs=[apart] * 3 + [whole] + [apart] * 2,
        out_specs=whole,
        scratch_shapes=[
            held(all_coils, rows, packed),
            held(frames, rows, packed),
            pltpu.VMEM(row_pairs.shape, jnp.bfloat16),
            pltpu.VMEM(col_pair.shape, jnp.bfloat16),
            held(pairs, 2, length // 2, packed),
            held(frames, 2 * length),
            held(coils, frames, length, packed),
            held(coils, length, packed),
            held(devices, rows, lanes),
            held(devices, rows, lanes),
            held(2, 2, all_coils // 2, width, length),
            held(2, frames, width, length),
            held(2, frames, width, length),
            pltpu.VMEM((frames, 2, 2, length, length), jnp.bfloat16),
            held(devices // 2, 2, coils, width, length // 2),
            held(frames, 2 * width, length),
            held(devices, rows, 2 * frames * width),
            held(devices, rows, 2 * frames * width),
            *sums,
            *gots,
            dma((all_coils + frames + 2,)),
            dma((pairs, 2)),
            dma((devices - 1, coils)),
            dma((devices - 1, coils)),
            dma((devices - 1,)),
            dma((devices - 1,)),
            dma((devices // 2 - 1,)),
            dma((devices // 2 - 1,)),
            dma((2, frames, bits)),
            dma((2, frames, bits)),
            dma((devices - 1,)),
            dma((devices - 1,)),
        ],
        compiler_params=pltpu.CompilerParams(
            collective_id=0, has_side_effects=True, vmem_limit_bytes=60 * 1024 * 1024
        ),
        name="reconstruct",
    )(
        image,
        sens,
        kspace.reshape(length // 2, 2, pairs, packed),
        mask,
        jnp.asarray(row_pairs),
        jnp.asarray(col_pair),
    )


def per_device(image, sens, kspace, mask):
    devices = lax.axis_size("coil")
    device = lax.axis_index("coil")
    rows_dev, frames, packed = image.shape
    coils = sens.shape[1]
    length, pairs, unused = kspace.shape
    half = packed // 2
    width = half // devices
    copies = max(1, frames // pairs)
    own_coils = max(1, pairs // frames)
    own_frames = min(frames, pairs)
    if blocked(devices, width, rows_dev, length, half, coils, frames, pairs):
        return reconstruct(image, sens, kspace, mask, devices)
    row_cos, row_sin = dft_tables(length)
    col_cos, col_sin = dft_tables(half)
    mask_float = mask.astype(jnp.float32)
    real, imag = projections(mask, row_cos, row_sin)
    spread = sens if copies == 1 else jnp.repeat(sens, copies, axis=1)
    own_maps = lax.all_to_all(spread, "coil", split_axis=1, concat_axis=0, tiled=True)
    outgoing = jnp.concatenate([to_columns(sens, devices), to_columns(image, devices)], 2)
    incoming = lax.all_to_all(outgoing, "coil", split_axis=0, concat_axis=0, tiled=True)
    columns = jnp.transpose(incoming.reshape(length, -1))
    first_frame = device * pairs % frames
    local_mask = lax.dynamic_slice_in_dim(mask_float, first_frame, own_frames, 0)
    mask_pairs = jnp.tile(local_mask, (own_coils, 1))
    base_re, base_im = data_images(kspace, mask_pairs, row_cos, row_sin, col_cos, col_sin)
    base_re = base_re.reshape(length, own_coils, own_frames, half)
    base_im = base_im.reshape(length, own_coils, own_frames, half)
    own_re, own_im = (own_maps[:, :, None, :half], own_maps[:, :, None, half:])
    term_re = jnp.sum(own_re * base_re + own_im * base_im, 1)
    term_im = jnp.sum(own_re * base_im - own_im * base_re, 1)
    term = jnp.transpose(jnp.stack([term_re, term_im]), (3, 0, 2, 1))
    if own_frames < frames:
        wide = jnp.zeros((half, 2, frames, length), jnp.float32)
        term = lax.dynamic_update_slice_in_dim(wide, term, first_frame, 2)
    term = term.reshape(devices, width, 2, frames, length)
    data_term = lax.psum_scatter(term, "coil", scatter_dimension=0, tiled=True)
    data_term = jnp.transpose(data_term[0], (1, 2, 0, 3))

    cut = 2 * coils * width
    maps = columns[:cut].reshape(2, coils, width, length)
    field = columns[cut:].reshape(2, frames, width, length)
    field = iterate(field, data_term, maps, real, imag)

    leaving = jnp.transpose(field.reshape(2 * frames * width, length))
    leaving = leaving.reshape(devices, rows_dev, 2 * frames * width)
    arrived = lax.all_to_all(leaving, "coil", split_axis=0, concat_axis=0, tiled=True)
    arrived = arrived.reshape(devices, rows_dev, 2, frames, width)
    return jnp.transpose(arrived, (1, 3, 2, 0, 4)).reshape(rows_dev, frames, packed)


def solution(mesh):
    return jax.shard_map(
        per_device,
        mesh=mesh,
        in_specs=(
            P(("plane", "coil"), None, None),
            P(("plane", "coil"), None, None),
            P("plane", "coil", None),
            P(),
        ),
        out_specs=P(("plane", "coil"), None, None),
        check_vma=False,
    )
```

```python
import jax
import jax.numpy as jnp
import numpy as np
from jax import lax
from jax.experimental import pallas as pl
from jax.experimental.pallas import tpu as pltpu
from jax.sharding import PartitionSpec as P

OUTER = 2
INNER = 2

step_size = 0.5
tv_weight = 0.1
dual_step = 1.25
high = lax.Precision.HIGH


def contract(spec, *operands):
    return jnp.einsum(spec, *operands, precision=high, preferred_element_type=jnp.float32)


def dft_tables(length):
    index = lax.iota(jnp.int32, length)
    product = index[:, None] * index[None, :] % length
    angle = 2.0 * jnp.pi / length * product.astype(jnp.float32)
    scale = 1.0 / jnp.sqrt(jnp.float32(length))
    return (jnp.cos(angle) * scale, -jnp.sin(angle) * scale)


def column_matrix(cos_part, sin_part):
    upper = jnp.concatenate([cos_part, sin_part], 1)
    lower = jnp.concatenate([-sin_part, cos_part], 1)
    return jnp.concatenate([upper, lower], 0)


def projections(mask, row_cos, row_sin):
    weights = mask.astype(jnp.float32)
    wide = jnp.concatenate([row_cos, row_sin], 1)
    cos_rows = weights[:, :, None] * row_cos[None]
    sin_rows = weights[:, :, None] * row_sin[None]
    from_cos = contract("fka,ky->fay", cos_rows, wide)
    from_sin = contract("fka,ky->fay", sin_rows, wide)
    length = row_cos.shape[0]
    real = from_cos[..., :length] + from_sin[..., length:]
    imag = from_cos[..., length:] - from_sin[..., :length]
    return (real, imag)


def to_columns(field, devices):
    rows, count, packed = field.shape
    width = packed // 2 // devices
    parts = field.reshape(rows, count, 2, devices, width)
    return jnp.transpose(parts, (3, 0, 2, 1, 4)).reshape(devices, rows, 2 * count * width)


def divergence(dual_time, dual_rows):
    time_axis, row_axis = 1, 3
    zero_time = jnp.zeros_like(dual_time[:, :1])
    zero_rows = jnp.zeros_like(dual_rows[..., :1])
    head_time = dual_time[:, :-1]
    head_rows = dual_rows[..., :-1]
    from_time = jnp.concatenate([zero_time, head_time], time_axis) - jnp.concatenate(
        [head_time, zero_time], time_axis
    )
    from_rows = jnp.concatenate([zero_rows, head_rows], row_axis) - jnp.concatenate(
        [head_rows, zero_rows], row_axis
    )
    return from_time + from_rows


def forward_diff(field):
    diff_time = jnp.concatenate(
        [field[:, 1:] - field[:, :-1], jnp.zeros_like(field[:, :1])], 1
    )
    diff_rows = jnp.concatenate(
        [field[..., 1:] - field[..., :-1], jnp.zeros_like(field[..., :1])], 3
    )
    return (diff_time, diff_rows)


def denoise(target):
    dual_time = jnp.zeros_like(target)
    dual_rows = jnp.zeros_like(target)
    for repeat in range(INNER):
        primal = target
        if repeat:
            primal = target - tv_weight * divergence(dual_time, dual_rows)
        diff_time, diff_rows = forward_diff(primal)
        dual_time = jnp.clip(dual_time + dual_step * diff_time, -1.0, 1.0)
        dual_rows = jnp.clip(dual_rows + dual_step * diff_rows, -1.0, 1.0)
    return target - tv_weight * divergence(dual_time, dual_rows)


def iterate(field, data_term, maps, real, imag):
    maps_re, maps_im = (maps[0][None], maps[1][None])
    for sweep in range(OUTER):
        now_re, now_im = (field[0][:, None], field[1][:, None])
        seen_re = maps_re * now_re - maps_im * now_im
        seen_im = maps_re * now_im + maps_im * now_re
        kept_re = contract("fczy,fky->fczk", seen_re, real) - contract(
            "fczy,fky->fczk", seen_im, imag
        )
        kept_im = contract("fczy,fky->fczk", seen_re, imag) + contract(
            "fczy,fky->fczk", seen_im, real
        )
        grad_re = jnp.sum(maps_re * kept_re + maps_im * kept_im, 1)
        grad_im = jnp.sum(maps_re * kept_im - maps_im * kept_re, 1)
        gradient = jnp.stack([grad_re, grad_im]) - data_term
        field = denoise(field - step_size * gradient)
    return field


def data_images(kspace, mask_pairs, row_cos, row_sin, col_cos, col_sin):
    masked = jnp.transpose(mask_pairs)[:, :, None] * kspace
    mid = contract("kpz,zw->kpw", masked, column_matrix(col_cos, -col_sin))
    half = kspace.shape[-1] // 2
    from_cos = contract("ky,kpz->ypz", row_cos, mid)
    from_sin = contract("ky,kpz->ypz", row_sin, mid)
    real = from_cos[..., :half] + from_sin[..., half:]
    imag = from_cos[..., half:] - from_sin[..., :half]
    return (real, imag)


LANES = 128
SUBLANES = 8


def swap_blocks(values, width):
    count = len(values)
    block = lax.broadcasted_iota(jnp.int32, values[0].shape, 1) // width
    step = count // 2
    while step:
        lower = block // step % 2 == 0
        shift = step * width
        values = list(values)
        for at in range(count):
            if at // step % 2 == 0:
                near, far = (values[at], values[at + step])
                values[at] = jnp.where(lower, near, pltpu.roll(far, shift, 1))
                values[at + step] = jnp.where(lower, pltpu.roll(near, LANES - shift, 1), far)
        step //= 2
    return values


def blocked(devices, width, rows, length, half, coils, frames, pairs):
    group = LANES // width
    fits = LANES % width == 0 and width % SUBLANES == 0 and rows % SUBLANES == 0
    fits = fits and devices % group == 0 and coils % (2 * group) == 0 and frames % group == 0
    fits = fits and devices & (devices - 1) == 0
    fits = fits and devices >= 16 and frames % 2 == 0 and pairs % frames == 0 and coils * frames == pairs * devices
    return fits and length % (2 * LANES) == 0 and half % (2 * LANES) == 0


def pack_kernel(devices, width, sens_ref, image_ref, out_ref):
    group = LANES // width
    half = devices * width
    near = sens_ref.shape[0] // 2
    start = 0
    for source, origin, count in (
        (sens_ref, 0, near),
        (image_ref, 0, image_ref.shape[0]),
        (sens_ref, near, near),
    ):
        for part in range(2):
            for tile in range(half // LANES):
                lane = part * half + tile * LANES
                for first in range(0, count, group):
                    taken = [
                        source[origin + first + at, :, lane : lane + LANES] for at in range(group)
                    ]
                    target = start + (part * count + first) * width
                    for at, value in enumerate(swap_blocks(taken, width)):
                        out_ref[tile * group + at, :, target : target + LANES] = value
        start += 2 * count * width


def split(value):
    top = value.astype(jnp.bfloat16)
    return (top, (value - top.astype(jnp.float32)).astype(jnp.bfloat16))


def narrow(value):
    value = value.astype(np.float32)
    top = value.astype(jnp.bfloat16)
    return np.stack([top, (value - top.astype(np.float32)).astype(jnp.bfloat16)])


def mix_left(value):
    top, low = split(value)
    return jnp.concatenate([low, top, top], 1)


def mix_right(pair):
    return jnp.concatenate([pair[0], pair[1], pair[0]], 0)


def dot(left, right):
    return jnp.dot(left, right, preferred_element_type=jnp.float32)


def row_tables(length):
    half = length // 2
    tables = []
    for odd in range(2):
        product = np.outer(np.arange(half), 2 * np.arange(half) + odd) % length
        angle = 2.0 * np.pi / length * product
        cos_part, sin_part = (np.cos(angle) / np.sqrt(length), np.sin(angle) / np.sqrt(length))
        tables.append(narrow(np.block([[cos_part, -sin_part], [sin_part, cos_part]])))
    return np.stack(tables)


def column_table(length):
    angle = 2.0 * np.pi / length * (np.outer(np.arange(length), np.arange(length)) % length)
    cos_part, sin_part = (np.cos(angle) / np.sqrt(length), np.sin(angle) / np.sqrt(length))
    return narrow(np.block([[cos_part, sin_part], [-sin_part, cos_part]]))


MESH = pl.DeviceIdType.MESH


def announce(peers):
    for peer in peers:
        pl.semaphore_signal(
            pltpu.get_barrier_semaphore(), 1, device_id={"coil": peer}, device_id_type=MESH
        )


def drain(whole, sem):
    pltpu.make_async_copy(whole, whole, sem).wait()


def shift_rows(value, step):
    length = value.shape[1]
    rolled = pltpu.roll(value, step % length, 1)
    at = lax.broadcasted_iota(jnp.int32, value.shape, 1)
    kept = at >= step if step > 0 else at < length + step
    return jnp.where(kept, rolled, 0.0)


def spread_rows(dual):
    return shift_rows(dual, 1) - dual


def row_steps(primal):
    length = primal.shape[1]
    at = lax.broadcasted_iota(jnp.int32, primal.shape, 1)
    return jnp.where(at < length - 1, pltpu.roll(primal, length - 1, 1) - primal, 0.0)


def clipped(value):
    return jnp.minimum(jnp.maximum(value, -1.0), 1.0)


def denoise_frames(target):
    frames = len(target)
    dual_time = [None] * frames
    dual_rows = [None] * frames

    def lowered(frame):
        moved = spread_rows(dual_rows[frame])
        if frame > 0:
            moved = moved + dual_time[frame - 1]
        if frame < frames - 1:
            moved = moved - dual_time[frame]
        return target[frame] - tv_weight * moved

    primal = target
    for repeat in range(INNER):
        if repeat:
            primal = [lowered(frame) for frame in range(frames)]
        for frame in range(frames):
            rows = dual_step * row_steps(primal[frame])
            dual_rows[frame] = clipped(rows if not repeat else dual_rows[frame] + rows)
            if frame < frames - 1:
                time = dual_step * (primal[frame + 1] - primal[frame])
                dual_time[frame] = clipped(time if not repeat else dual_time[frame] + time)
    return [lowered(frame) for frame in range(frames)]


def whole_kernel(
    devices,
    image_ref,
    sens_ref,
    kspace_ref,
    mask_ref,
    rows_ref,
    cols_ref,
    out_ref,
    sens_v,
    image_v,
    rows_v,
    cols_v,
    data_ref,
    mask_v,
    base_ref,
    maps_ref,
    packed_ref,
    landed_ref,
    own_ref,
    now_ref,
    grad_ref,
    gram_ref,
    relay_ref,
    total_ref,
    ready_ref,
    back_ref,
    *rest,
):
    bits = devices.bit_length() - 1
    sums = rest[:bits]
    gots = rest[bits : 2 * bits]
    (
        load_sem,
        maps_send,
        maps_recv,
        pack_send,
        pack_recv,
        relay_send,
        relay_recv,
        sum_send,
        sum_recv,
        back_send,
        back_recv,
    ) = rest[2 * bits :]
    coils, frames, length, packed = base_ref.shape
    rows, all_coils, unused = sens_ref.shape
    half = packed // 2
    low = length // 2
    width = half // devices
    group = LANES // width
    me = lax.axis_index("coil")
    own_bits = [me // (1 << bit) % 2 for bit in range(bits)]
    peers = []
    for hop in range(1, devices):
        flips = [(own_bits[bit] + (hop >> bit)) % 2 * (1 << bit) for bit in range(bits)]
        peers.append(sum(flips[1:], flips[0]))
    near = devices // 2
    some = frames // 2
    side = me // near
    far_side = 1 - side
    near_hops = list(range(1, near))
    far_hops = list(range(near, devices))
    block = all_coils * width
    held_lanes = 2 * frames * width
    own_rows = pl.ds(pl.multiple_of(me * rows, SUBLANES), rows)

    announce(peers)
    for coil in range(all_coils):
        pltpu.make_async_copy(sens_ref.at[:, coil, :], sens_v.at[coil], load_sem.at[0]).start()
    for frame in range(frames):
        pltpu.make_async_copy(image_ref.at[:, frame, :], image_v.at[frame], load_sem.at[1]).start()
    pltpu.make_async_copy(rows_ref, rows_v, load_sem.at[2]).start()
    pltpu.make_async_copy(cols_ref, cols_v, load_sem.at[3]).start()
    for pair in range(coils * frames):
        for odd in range(2):
            pltpu.make_async_copy(
                kspace_ref.at[:, odd, pair, :], data_ref.at[pair, odd], load_sem.at[4]
            ).start()

    def remote(source, target, send, recv, peer):
        return pltpu.make_async_remote_copy(
            src_ref=source,
            dst_ref=target,
            send_sem=send,
            recv_sem=recv,
            device_id={"coil": peer},
            device_id_type=MESH,
        )

    def maps_copy(hop, coil):
        peer = peers[hop - 1]
        return remote(
            sens_ref.at[:, peer * coils + coil, :],
            maps_ref.at[coil, own_rows, :],
            maps_send.at[0],
            maps_recv.at[hop // near],
            peer,
        )

    def pack_copy(hop):
        peer = peers[hop - 1]
        if hop < near:
            lanes = pl.ds(0, 2 * block + held_lanes)
        else:
            lanes = pl.ds(pl.multiple_of(side * block, LANES), block + held_lanes)
        return remote(
            packed_ref.at[peer, :, lanes],
            landed_ref.at[me, :, lanes],
            pack_send.at[hop // near],
            pack_recv.at[hop // near],
            peer,
        )

    def relay_part(coil_side, first, row_side):
        lanes = pl.ds(pl.multiple_of(row_side * low, LANES), low)
        return own_ref.at[coil_side, :, pl.ds(first, coils), :, lanes]

    def relay_copy(hop):
        peer = peers[hop - 1]
        return remote(
            relay_ref.at[peer % near],
            relay_part(side, me % near * coils, far_side),
            relay_send.at[0],
            relay_recv.at[0],
            peer,
        )

    def kept_part(stage, phase, frame, other):
        at = own_bits[stage]
        at = 1 - at if other else at
        lead = (slice(None),) * (bits - 1 - stage)
        return sums[stage].at[(phase, frame) + lead + (at,)]

    def sum_copy(stage, phase, frame):
        landing = 1 - phase if stage == bits - 1 else phase
        return remote(
            kept_part(stage, phase, frame, True),
            gots[stage].at[landing, frame],
            sum_send.at[stage],
            sum_recv.at[landing, frame, stage],
            me + (1 - 2 * own_bits[stage]) * (1 << stage),
        )

    def side_rows(phase):
        row_side = far_side if phase else side
        return pl.ds(pl.multiple_of(row_side * low, LANES), low)

    def collect(stage, phase, frame):
        last = stage == bits - 1
        sum_copy(stage, 1 - phase if last else phase, frame).wait_recv()
        total = kept_part(stage, phase, frame, False)[...] + gots[stage][phase, frame]
        if last:
            total_ref[frame, :, side_rows(phase)] = total
        else:
            sums[stage + 1][phase, frame] = total

    pl.semaphore_wait(pltpu.get_barrier_semaphore(), len(peers))
    early = near // 2
    for hop in near_hops + far_hops[:early]:
        for coil in range(coils):
            maps_copy(hop, coil).start()
    drain(sens_v, load_sem.at[0])
    drain(image_v, load_sem.at[1])
    pack_kernel(devices, width, sens_v, image_v, packed_ref)
    for at in range(near - 1):
        if at < early:
            for coil in range(coils):
                maps_copy(far_hops[early + at], coil).start()
        pack_copy(near_hops[at]).start()
    for hop in far_hops:
        if hop // 2 % 2 == 0:
            pack_copy(hop).start()
    for coil in range(coils):
        maps_ref[coil, own_rows, :] = sens_v[me * coils + coil]
    landed_ref[me] = packed_ref[me]

    lane = lax.broadcasted_iota(jnp.int32, (length, 2 * length), 1)
    line = lax.broadcasted_iota(jnp.int32, (length, 2 * length), 0)
    picked = line == 2 * (lane % low) + lane // length
    mask_v[...] = dot(
        mask_ref[...].astype(jnp.float32).astype(jnp.bfloat16),
        jnp.where(picked, 1.0, 0.0).astype(jnp.bfloat16),
    )
    drain(rows_v, load_sem.at[2])
    drain(cols_v, load_sem.at[3])
    drain(data_ref, load_sem.at[4])

    def transform(frame):
        mixes = []
        for odd in range(2):
            weight = mask_v[pl.ds(frame, 1), odd * length : (odd + 1) * length].astype(jnp.bfloat16)
            top, rest_part = (rows_v[odd, 0] * weight, rows_v[odd, 1] * weight)
            mixes.append(jnp.concatenate([rest_part, top, top], 1))
            right = jnp.concatenate([rows_v[odd, 0], rows_v[odd, 1], rows_v[odd, 0]], 1)
            gram = lax.dot_general(
                mixes[-1], right, (((1,), (1,)), ((), ())), preferred_element_type=jnp.float32
            )
            top, rest_part = split(gram)
            gram_ref[frame, odd, 0] = top
            gram_ref[frame, odd, 1] = rest_part
        for coil in range(coils):
            parts = []
            for odd in range(2):
                lines = data_ref[coil * frames + frame, odd]
                lines = jnp.concatenate([lines[:, :half], lines[:, half:]], 0)
                parts.append(dot(mixes[odd], mix_right(split(lines))))
            near, far = (parts[0] + parts[1], parts[0] - parts[1])
            mid = jnp.concatenate(
                [
                    jnp.concatenate([near[:low], near[low:]], 1),
                    jnp.concatenate([far[:low], far[low:]], 1),
                ],
                0,
            )
            base_ref[coil, frame] = dot(mix_left(mid), mix_right(cols_v))

    def weigh(phase, frame):
        real, imag = (0.0, 0.0)
        lines = side_rows(phase)
        for coil in range(coils):
            base_re, base_im = (
                base_ref[coil, frame, lines, :half],
                base_ref[coil, frame, lines, half:],
            )
            maps_re, maps_im = (maps_ref[coil, lines, :half], maps_ref[coil, lines, half:])
            real = real + maps_re * base_re + maps_im * base_im
            imag = imag + maps_re * base_im - maps_im * base_re
        shape = (2,) * bits + (width, low)
        lead = (phase, frame) + (slice(None),) * bits
        sums[0][lead + (slice(0, width),)] = jnp.transpose(real).reshape(shape)
        sums[0][lead + (slice(width, 2 * width),)] = jnp.transpose(imag).reshape(shape)

    def pass_on(stage, phase, frame):
        if 0 <= frame < frames:
            collect(stage, phase, frame)
            sum_copy(stage + 1, phase, frame).start()

    def offer(phase, frame):
        if frame < frames:
            weigh(phase, frame)
            sum_copy(0, phase, frame).start()
        pass_on(0, phase, frame - 1)

    lead = min(3, frames - 1)

    def step(frame, unused):
        transform(frame)

        @pl.when(frame == lead)
        def wait_near():
            drain(maps_ref.at[:, pl.ds(0, (near - 1) * rows), :], maps_recv.at[0])

        @pl.when(frame >= lead)
        def offer_near():
            weigh(0, frame - lead)
            sum_copy(0, 0, frame - lead).start()

        @pl.when(frame > lead)
        def pass_near():
            collect(0, 0, frame - lead - 1)
            sum_copy(1, 0, frame - lead - 1).start()

        return unused

    lax.fori_loop(0, frames, step, 0)
    for turn in range(frames - lead, frames + 1):
        offer(0, turn)
    for hop in far_hops:
        if hop // 2 % 2:
            pack_copy(hop).start()
    drain(maps_ref.at[:, pl.ds(0, near * rows), :], maps_recv.at[1])

    def project(sweep, frame):
        shape = (all_coils, width, length)
        maps_re, maps_im = (own_ref[:, 0].reshape(shape), own_ref[:, 1].reshape(shape))
        now_re, now_im = (now_ref[sweep, 0, frame][None], now_ref[sweep, 1, frame][None])
        seen_re = (maps_re * now_re - maps_im * now_im).reshape(all_coils * width, length)
        seen_im = (maps_re * now_im + maps_im * now_re).reshape(all_coils * width, length)
        parts = []
        for odd in range(2):
            if odd:
                both = [part[:, :low] - part[:, low:] for part in (seen_re, seen_im)]
            else:
                both = [part[:, :low] + part[:, low:] for part in (seen_re, seen_im)]
            parts.append(dot(mix_left(jnp.concatenate(both, 1)), mix_right(gram_ref[frame, odd])))
        near, far = (parts[0] + parts[1], parts[0] - parts[1])
        kept_re = jnp.concatenate([near[:, :low], far[:, :low]], 1).reshape(shape)
        kept_im = jnp.concatenate([near[:, low:], far[:, low:]], 1).reshape(shape)
        grad_ref[sweep, 0, frame] = jnp.sum(maps_re * kept_re + maps_im * kept_im, 0)
        grad_ref[sweep, 1, frame] = jnp.sum(maps_re * kept_im - maps_im * kept_re, 0)

    def turn_maps():
        lines = pl.ds(pl.multiple_of(far_side * low, LANES), low)
        for coil in range(coils):
            for part in range(2):
                lanes = pl.ds(pl.multiple_of(part * half + side * (half // 2), LANES), half // 2)
                turned = jnp.transpose(maps_ref[coil, lines, lanes])
                relay_ref[:, part, coil] = turned.reshape(near, width, low)
        for hop in near_hops:
            relay_copy(hop).start()
        relay_part(side, me % near * coils, far_side)[...] = relay_ref[me % near]

    def unfold(target, row_side, lines, lanes):
        turned = jnp.transpose(landed_ref[lines, :, lanes].reshape(low, -1))
        rows_at = pl.ds(pl.multiple_of(row_side * low, LANES), low)
        target[..., rows_at] = turned.reshape(target.shape[:-1] + (low,))

    def take_columns():
        drain(landed_ref.at[pl.ds(0, near - 1)], pack_recv.at[0])
        drain(landed_ref.at[pl.ds(0, near), :, pl.ds(0, block + held_lanes)], pack_recv.at[1])
        drain(relay_ref.at[pl.ds(0, near - 1)], relay_recv.at[0])
        for row_side in (side, far_side):
            lines = pl.ds(row_side * near, near)
            unfold(now_ref.at[0], row_side, lines, pl.ds(block, held_lanes))
        for coil_side, row_side in ((0, side), (1, side), (far_side, far_side)):
            start = pl.multiple_of(coil_side * (block + held_lanes), LANES)
            lines = pl.ds(row_side * near, near)
            unfold(own_ref.at[coil_side], row_side, lines, pl.ds(start, block))

    for turn in range(frames + 1):
        offer(1, turn)
        if turn == 0:
            turn_maps()
        pass_on(1, 0, turn)
    projected = [0] * OUTER
    settled = [0] * OUTER
    summed = [0]

    def project_to(sweep, count):
        while projected[sweep] < min(count, frames):
            if sweep and projected[sweep] == settled[sweep - 1]:
                advance(sweep - 1)
            project(sweep, projected[sweep])
            projected[sweep] += 1

    def back_copy(piece, hop):
        peer = peers[hop - 1]
        return remote(
            ready_ref.at[piece, peer],
            back_ref.at[piece, me],
            back_send.at[piece],
            back_recv.at[piece],
            peer,
        )

    def settle(sweep, part, start, stop):
        first = max(0, start - INNER)
        target = []
        for frame in range(first, min(frames, stop + INNER)):
            data_term = total_ref[frame, part * width : (part + 1) * width]
            gradient = grad_ref[sweep, part, frame] - data_term
            target.append(now_ref[sweep, part, frame] - step_size * gradient)
        return denoise_frames(target)[start - first : stop - first]

    def advance(sweep):
        start = settled[sweep]
        stop = start + (some if sweep == OUTER - 1 else max(1, some // 2))
        project_to(sweep, stop + INNER)
        while summed[0] < min(frames, stop + INNER):
            for phase in range(2):
                collect(bits - 1, phase, summed[0])
            summed[0] += 1
        parts = [settle(sweep, part, start, stop) for part in range(2)]
        settled[sweep] = stop
        if sweep < OUTER - 1:
            for part in range(2):
                for frame, value in enumerate(parts[part]):
                    now_ref[sweep + 1, part, start + frame] = value
            return
        piece = start // some
        turned = jnp.transpose(jnp.concatenate(parts[0] + parts[1], 0))
        ready_ref[piece] = turned.reshape(ready_ref.shape[1:])
        for hop in far_hops + near_hops:
            back_copy(piece, hop).start()
        back_ref[piece, me] = ready_ref[piece, me]

    for turn in range(frames):
        pass_on(1, 1, turn)
        pass_on(2, 0, turn)
        pass_on(2, 1, turn - 2)
        if turn == 1:
            take_columns()
        project_to(0, turn)

    for frame in range(frames - 2, frames):
        if bits == 4:
            project_to(1, frame + 3 - frames)
        pass_on(2, 1, frame)
    for stage in range(3, bits - 1):
        for phase in range(2):
            for frame in range(frames):
                pass_on(stage, phase, frame)

    for piece in range(2):
        advance(OUTER - 1)
    for piece in range(2):
        drain(back_ref.at[piece, pl.ds(0, devices - 1)], back_recv.at[piece])
        for first in range(0, frames, group):
            for tile in range(devices // group):
                taken = [
                    back_ref[piece, tile * group + at, :, first * width : first * width + LANES]
                    for at in range(group)
                ]
                for at, value in enumerate(swap_blocks(taken, width)):
                    part, frame = ((first + at) // some, piece * some + (first + at) % some)
                    target = part * half + tile * LANES
                    out_ref[:, frame, target : target + LANES] = value
    drain(maps_ref.at[:, pl.ds(0, (devices - 1) * rows), :], maps_send.at[0])
    drain(landed_ref.at[pl.ds(0, near - 1)], pack_send.at[0])
    drain(landed_ref.at[pl.ds(0, near), :, pl.ds(0, block + held_lanes)], pack_send.at[1])
    drain(relay_ref.at[pl.ds(0, near - 1)], relay_send.at[0])
    for piece in range(2):
        drain(back_ref.at[piece, pl.ds(0, devices - 1)], back_send.at[piece])
    for stage in range(bits):
        drain(gots[stage], sum_send.at[stage])


def reconstruct(image, sens, kspace, mask, devices):
    rows, frames, packed = image.shape
    all_coils = sens.shape[1]
    length, pairs, unused = kspace.shape
    coils = pairs // frames
    bits = devices.bit_length() - 1
    width = packed // 2 // devices
    lanes = 2 * (all_coils + frames) * width
    row_pairs = row_tables(length)
    col_pair = column_table(packed // 2)
    whole = pl.BlockSpec(memory_space=pltpu.VMEM)
    apart = pl.BlockSpec(memory_space=pl.ANY)

    def held(*shape):
        return pltpu.VMEM(shape, jnp.float32)

    dma = pltpu.SemaphoreType.DMA
    block = (2 * width, length // 2)
    sums = [held(2, frames, *(2,) * (bits - stage), *block) for stage in range(bits)]
    gots = [held(2, frames, *(2,) * (bits - 1 - stage), *block) for stage in range(bits)]
    return pl.pallas_call(
        lambda *refs: whole_kernel(devices, *refs),
        out_shape=jax.ShapeDtypeStruct((rows, frames, packed), jnp.float32),
        in_specs=[apart] * 3 + [whole] + [apart] * 2,
        out_specs=whole,
        scratch_shapes=[
            held(all_coils, rows, packed),
            held(frames, rows, packed),
            pltpu.VMEM(row_pairs.shape, jnp.bfloat16),
            pltpu.VMEM(col_pair.shape, jnp.bfloat16),
            held(pairs, 2, length // 2, packed),
            held(frames, 2 * length),
            held(coils, frames, length, packed),
            held(coils, length, packed),
            held(devices, rows, lanes),
            held(devices, rows, lanes),
            held(2, 2, all_coils // 2, width, length),
            held(OUTER, 2, frames, width, length),
            held(OUTER, 2, frames, width, length),
            pltpu.VMEM((frames, 2, 2, length, length), jnp.bfloat16),
            held(devices // 2, 2, coils, width, length // 2),
            held(frames, 2 * width, length),
            held(2, devices, rows, frames * width),
            held(2, devices, rows, frames * width),
            *sums,
            *gots,
            dma((5,)),
            dma((1,)),
            dma((2,)),
            dma((2,)),
            dma((2,)),
            dma((1,)),
            dma((1,)),
            dma((bits,)),
            dma((2, frames, bits)),
            dma((2,)),
            dma((2,)),
        ],
        compiler_params=pltpu.CompilerParams(
            collective_id=0, has_side_effects=True, vmem_limit_bytes=60 * 1024 * 1024
        ),
        name="reconstruct",
    )(
        image,
        sens,
        kspace.reshape(length // 2, 2, pairs, packed),
        mask,
        jnp.asarray(row_pairs),
        jnp.asarray(col_pair),
    )


def per_device(image, sens, kspace, mask):
    devices = lax.axis_size("coil")
    device = lax.axis_index("coil")
    rows_dev, frames, packed = image.shape
    coils = sens.shape[1]
    length, pairs, unused = kspace.shape
    half = packed // 2
    width = half // devices
    copies = max(1, frames // pairs)
    own_coils = max(1, pairs // frames)
    own_frames = min(frames, pairs)
    if blocked(devices, width, rows_dev, length, half, coils, frames, pairs):
        return reconstruct(image, sens, kspace, mask, devices)
    row_cos, row_sin = dft_tables(length)
    col_cos, col_sin = dft_tables(half)
    mask_float = mask.astype(jnp.float32)
    real, imag = projections(mask, row_cos, row_sin)
    spread = sens if copies == 1 else jnp.repeat(sens, copies, axis=1)
    own_maps = lax.all_to_all(spread, "coil", split_axis=1, concat_axis=0, tiled=True)
    outgoing = jnp.concatenate([to_columns(sens, devices), to_columns(image, devices)], 2)
    incoming = lax.all_to_all(outgoing, "coil", split_axis=0, concat_axis=0, tiled=True)
    columns = jnp.transpose(incoming.reshape(length, -1))
    first_frame = device * pairs % frames
    local_mask = lax.dynamic_slice_in_dim(mask_float, first_frame, own_frames, 0)
    mask_pairs = jnp.tile(local_mask, (own_coils, 1))
    base_re, base_im = data_images(kspace, mask_pairs, row_cos, row_sin, col_cos, col_sin)
    base_re = base_re.reshape(length, own_coils, own_frames, half)
    base_im = base_im.reshape(length, own_coils, own_frames, half)
    own_re, own_im = (own_maps[:, :, None, :half], own_maps[:, :, None, half:])
    term_re = jnp.sum(own_re * base_re + own_im * base_im, 1)
    term_im = jnp.sum(own_re * base_im - own_im * base_re, 1)
    term = jnp.transpose(jnp.stack([term_re, term_im]), (3, 0, 2, 1))
    if own_frames < frames:
        wide = jnp.zeros((half, 2, frames, length), jnp.float32)
        term = lax.dynamic_update_slice_in_dim(wide, term, first_frame, 2)
    term = term.reshape(devices, width, 2, frames, length)
    data_term = lax.psum_scatter(term, "coil", scatter_dimension=0, tiled=True)
    data_term = jnp.transpose(data_term[0], (1, 2, 0, 3))

    cut = 2 * coils * width
    maps = columns[:cut].reshape(2, coils, width, length)
    field = columns[cut:].reshape(2, frames, width, length)
    field = iterate(field, data_term, maps, real, imag)

    leaving = jnp.transpose(field.reshape(2 * frames * width, length))
    leaving = leaving.reshape(devices, rows_dev, 2 * frames * width)
    arrived = lax.all_to_all(leaving, "coil", split_axis=0, concat_axis=0, tiled=True)
    arrived = arrived.reshape(devices, rows_dev, 2, frames, width)
    return jnp.transpose(arrived, (1, 3, 2, 0, 4)).reshape(rows_dev, frames, packed)


def solution(mesh):
    return jax.shard_map(
        per_device,
        mesh=mesh,
        in_specs=(
            P(("plane", "coil"), None, None),
            P(("plane", "coil"), None, None),
            P("plane", "coil", None),
            P(),
        ),
        out_specs=P(("plane", "coil"), None, None),
        check_vma=False,
    )
```

```python
import jax
import jax.numpy as jnp
import numpy as np
from jax import lax
from jax.experimental import pallas as pl
from jax.experimental.pallas import tpu as pltpu
from jax.sharding import PartitionSpec as P

OUTER = 2
INNER = 2

step_size = 0.5
tv_weight = 0.1
dual_step = 1.25
high = lax.Precision.HIGH


def contract(spec, *operands):
    return jnp.einsum(spec, *operands, precision=high, preferred_element_type=jnp.float32)


def dft_tables(length):
    index = lax.iota(jnp.int32, length)
    product = index[:, None] * index[None, :] % length
    angle = 2.0 * jnp.pi / length * product.astype(jnp.float32)
    scale = 1.0 / jnp.sqrt(jnp.float32(length))
    return (jnp.cos(angle) * scale, -jnp.sin(angle) * scale)


def column_matrix(cos_part, sin_part):
    upper = jnp.concatenate([cos_part, sin_part], 1)
    lower = jnp.concatenate([-sin_part, cos_part], 1)
    return jnp.concatenate([upper, lower], 0)


def projections(mask, row_cos, row_sin):
    weights = mask.astype(jnp.float32)
    wide = jnp.concatenate([row_cos, row_sin], 1)
    cos_rows = weights[:, :, None] * row_cos[None]
    sin_rows = weights[:, :, None] * row_sin[None]
    from_cos = contract("fka,ky->fay", cos_rows, wide)
    from_sin = contract("fka,ky->fay", sin_rows, wide)
    length = row_cos.shape[0]
    real = from_cos[..., :length] + from_sin[..., length:]
    imag = from_cos[..., length:] - from_sin[..., :length]
    return (real, imag)


def to_columns(field, devices):
    rows, count, packed = field.shape
    width = packed // 2 // devices
    parts = field.reshape(rows, count, 2, devices, width)
    return jnp.transpose(parts, (3, 0, 2, 1, 4)).reshape(devices, rows, 2 * count * width)


def divergence(dual_time, dual_rows):
    time_axis, row_axis = 1, 3
    zero_time = jnp.zeros_like(dual_time[:, :1])
    zero_rows = jnp.zeros_like(dual_rows[..., :1])
    head_time = dual_time[:, :-1]
    head_rows = dual_rows[..., :-1]
    from_time = jnp.concatenate([zero_time, head_time], time_axis) - jnp.concatenate(
        [head_time, zero_time], time_axis
    )
    from_rows = jnp.concatenate([zero_rows, head_rows], row_axis) - jnp.concatenate(
        [head_rows, zero_rows], row_axis
    )
    return from_time + from_rows


def forward_diff(field):
    diff_time = jnp.concatenate(
        [field[:, 1:] - field[:, :-1], jnp.zeros_like(field[:, :1])], 1
    )
    diff_rows = jnp.concatenate(
        [field[..., 1:] - field[..., :-1], jnp.zeros_like(field[..., :1])], 3
    )
    return (diff_time, diff_rows)


def denoise(target):
    dual_time = jnp.zeros_like(target)
    dual_rows = jnp.zeros_like(target)
    for repeat in range(INNER):
        primal = target
        if repeat:
            primal = target - tv_weight * divergence(dual_time, dual_rows)
        diff_time, diff_rows = forward_diff(primal)
        dual_time = jnp.clip(dual_time + dual_step * diff_time, -1.0, 1.0)
        dual_rows = jnp.clip(dual_rows + dual_step * diff_rows, -1.0, 1.0)
    return target - tv_weight * divergence(dual_time, dual_rows)


def iterate(field, data_term, maps, real, imag):
    maps_re, maps_im = (maps[0][None], maps[1][None])
    for sweep in range(OUTER):
        now_re, now_im = (field[0][:, None], field[1][:, None])
        seen_re = maps_re * now_re - maps_im * now_im
        seen_im = maps_re * now_im + maps_im * now_re
        kept_re = contract("fczy,fky->fczk", seen_re, real) - contract(
            "fczy,fky->fczk", seen_im, imag
        )
        kept_im = contract("fczy,fky->fczk", seen_re, imag) + contract(
            "fczy,fky->fczk", seen_im, real
        )
        grad_re = jnp.sum(maps_re * kept_re + maps_im * kept_im, 1)
        grad_im = jnp.sum(maps_re * kept_im - maps_im * kept_re, 1)
        gradient = jnp.stack([grad_re, grad_im]) - data_term
        field = denoise(field - step_size * gradient)
    return field


def data_images(kspace, mask_pairs, row_cos, row_sin, col_cos, col_sin):
    masked = jnp.transpose(mask_pairs)[:, :, None] * kspace
    mid = contract("kpz,zw->kpw", masked, column_matrix(col_cos, -col_sin))
    half = kspace.shape[-1] // 2
    from_cos = contract("ky,kpz->ypz", row_cos, mid)
    from_sin = contract("ky,kpz->ypz", row_sin, mid)
    real = from_cos[..., :half] + from_sin[..., half:]
    imag = from_cos[..., half:] - from_sin[..., :half]
    return (real, imag)


LANES = 128
SUBLANES = 8


def swap_blocks(values, width):
    count = len(values)
    block = lax.broadcasted_iota(jnp.int32, values[0].shape, 1) // width
    step = count // 2
    while step:
        lower = block // step % 2 == 0
        shift = step * width
        values = list(values)
        for at in range(count):
            if at // step % 2 == 0:
                near, far = (values[at], values[at + step])
                values[at] = jnp.where(lower, near, pltpu.roll(far, shift, 1))
                values[at + step] = jnp.where(lower, pltpu.roll(near, LANES - shift, 1), far)
        step //= 2
    return values


def blocked(devices, width, rows, length, half, coils, frames, pairs):
    group = LANES // width
    fits = LANES % width == 0 and width % SUBLANES == 0 and rows % SUBLANES == 0
    fits = fits and devices % group == 0 and coils % (2 * group) == 0 and frames % group == 0
    fits = fits and devices & (devices - 1) == 0
    fits = fits and devices >= 16 and frames % 2 == 0 and pairs % frames == 0 and coils * frames == pairs * devices
    return fits and length % (2 * LANES) == 0 and half % (2 * LANES) == 0


def pack_kernel(devices, width, sens_ref, image_ref, out_ref):
    group = LANES // width
    half = devices * width
    near = sens_ref.shape[0] // 2
    start = 0
    for source, origin, count in (
        (sens_ref, 0, near),
        (image_ref, 0, image_ref.shape[0]),
        (sens_ref, near, near),
    ):
        for part in range(2):
            for tile in range(half // LANES):
                lane = part * half + tile * LANES
                for first in range(0, count, group):
                    taken = [
                        source[origin + first + at, :, lane : lane + LANES] for at in range(group)
                    ]
                    target = start + (part * count + first) * width
                    for at, value in enumerate(swap_blocks(taken, width)):
                        out_ref[tile * group + at, :, target : target + LANES] = value
        start += 2 * count * width


def split(value):
    top = value.astype(jnp.bfloat16)
    return (top, (value - top.astype(jnp.float32)).astype(jnp.bfloat16))


def narrow(value):
    value = value.astype(np.float32)
    top = value.astype(jnp.bfloat16)
    return np.stack([top, (value - top.astype(np.float32)).astype(jnp.bfloat16)])


def mix_left(value):
    top, low = split(value)
    return jnp.concatenate([low, top, top], 1)


def mix_right(pair):
    return jnp.concatenate([pair[0], pair[1], pair[0]], 0)


def dot(left, right):
    return jnp.dot(left, right, preferred_element_type=jnp.float32)


def row_tables(length):
    half = length // 2
    tables = []
    for odd in range(2):
        product = np.outer(np.arange(half), 2 * np.arange(half) + odd) % length
        angle = 2.0 * np.pi / length * product
        cos_part, sin_part = (np.cos(angle) / np.sqrt(length), np.sin(angle) / np.sqrt(length))
        tables.append(narrow(np.block([[cos_part, -sin_part], [sin_part, cos_part]])))
    return np.stack(tables)


def column_table(length):
    angle = 2.0 * np.pi / length * (np.outer(np.arange(length), np.arange(length)) % length)
    cos_part, sin_part = (np.cos(angle) / np.sqrt(length), np.sin(angle) / np.sqrt(length))
    return narrow(np.block([[cos_part, sin_part], [-sin_part, cos_part]]))


MESH = pl.DeviceIdType.MESH


def announce(peers):
    for peer in peers:
        pl.semaphore_signal(
            pltpu.get_barrier_semaphore(), 1, device_id={"coil": peer}, device_id_type=MESH
        )


def drain(whole, sem):
    pltpu.make_async_copy(whole, whole, sem).wait()


def shift_rows(value, step):
    length = value.shape[1]
    rolled = pltpu.roll(value, step % length, 1)
    at = lax.broadcasted_iota(jnp.int32, value.shape, 1)
    kept = at >= step if step > 0 else at < length + step
    return jnp.where(kept, rolled, 0.0)


def spread_rows(dual):
    return shift_rows(dual, 1) - dual


def row_steps(primal):
    length = primal.shape[1]
    at = lax.broadcasted_iota(jnp.int32, primal.shape, 1)
    return jnp.where(at < length - 1, pltpu.roll(primal, length - 1, 1) - primal, 0.0)


def clipped(value):
    return jnp.minimum(jnp.maximum(value, -1.0), 1.0)


def whole_kernel(
    devices,
    image_ref,
    sens_ref,
    kspace_ref,
    mask_ref,
    rows_ref,
    cols_ref,
    out_ref,
    sens_v,
    image_v,
    rows_v,
    cols_v,
    data_ref,
    mask_v,
    base_ref,
    maps_ref,
    packed_ref,
    landed_ref,
    own_ref,
    now_ref,
    grad_ref,
    gram_ref,
    relay_ref,
    total_ref,
    ready_ref,
    back_ref,
    *rest,
):
    bits = devices.bit_length() - 1
    sums = rest[:bits]
    gots = rest[bits : 2 * bits]
    (
        load_sem,
        maps_send,
        maps_recv,
        pack_send,
        pack_recv,
        relay_send,
        relay_recv,
        sum_send,
        sum_recv,
        back_send,
        back_recv,
    ) = rest[2 * bits :]
    coils, frames, length, packed = base_ref.shape
    rows, all_coils, unused = sens_ref.shape
    half = packed // 2
    low = length // 2
    width = half // devices
    group = LANES // width
    me = lax.axis_index("coil")
    own_bits = [me // (1 << bit) % 2 for bit in range(bits)]
    inner = (own_bits[bits - 1] + own_bits[bits - 2]) % 2
    peers = []
    for hop in range(1, devices):
        turns = [hop >> bit for bit in range(bits)]
        if hop >= devices // 2:
            turns[bits - 2] += inner
        flips = [(own_bits[bit] + turns[bit]) % 2 * (1 << bit) for bit in range(bits)]
        peers.append(sum(flips[1:], flips[0]))
    near = devices // 2
    some = frames // 2
    side = me // near
    far_side = 1 - side
    near_hops = list(range(1, near))
    far_hops = list(range(near, devices))
    block = all_coils * width
    held_lanes = 2 * frames * width
    own_rows = pl.ds(pl.multiple_of(me * rows, SUBLANES), rows)

    announce(peers)
    for coil in range(all_coils):
        pltpu.make_async_copy(sens_ref.at[:, coil, :], sens_v.at[coil], load_sem.at[0]).start()
    for frame in range(frames):
        pltpu.make_async_copy(image_ref.at[:, frame, :], image_v.at[frame], load_sem.at[1]).start()
    pltpu.make_async_copy(rows_ref, rows_v, load_sem.at[2]).start()
    pltpu.make_async_copy(cols_ref, cols_v, load_sem.at[3]).start()
    for pair in range(coils * frames):
        for odd in range(2):
            pltpu.make_async_copy(
                kspace_ref.at[:, odd, pair, :], data_ref.at[pair, odd], load_sem.at[4]
            ).start()

    def remote(source, target, send, recv, peer):
        return pltpu.make_async_remote_copy(
            src_ref=source,
            dst_ref=target,
            send_sem=send,
            recv_sem=recv,
            device_id={"coil": peer},
            device_id_type=MESH,
        )

    def maps_copy(hop, coil):
        peer = peers[hop - 1]
        return remote(
            sens_ref.at[:, peer * coils + coil, :],
            maps_ref.at[coil, own_rows, :],
            maps_send.at[0],
            maps_recv.at[hop // near],
            peer,
        )

    def pack_copy(hop):
        peer = peers[hop - 1]
        if hop < near:
            lanes = pl.ds(0, 2 * block + held_lanes)
        else:
            lanes = pl.ds(pl.multiple_of(side * block, LANES), block + held_lanes)
        return remote(
            packed_ref.at[peer, :, lanes],
            landed_ref.at[me, :, lanes],
            pack_send.at[hop // near],
            pack_recv.at[hop // near],
            peer,
        )

    def relay_part(coil_side, first, row_side):
        lanes = pl.ds(pl.multiple_of(row_side * low, LANES), low)
        return own_ref.at[coil_side, :, pl.ds(first, coils), :, lanes]

    def relay_copy(hop):
        peer = peers[hop - 1]
        return remote(
            relay_ref.at[peer % near],
            relay_part(side, me % near * coils, far_side),
            relay_send.at[0],
            relay_recv.at[0],
            peer,
        )

    def kept_part(stage, phase, frame, other):
        at = own_bits[stage]
        at = 1 - at if other else at
        lead = (slice(None),) * (bits - 1 - stage)
        return sums[stage].at[(phase, frame) + lead + (at,)]

    def sum_copy(stage, phase, frame):
        landing = 1 - phase if stage == bits - 1 else phase
        return remote(
            kept_part(stage, phase, frame, True),
            gots[stage].at[landing, frame],
            sum_send.at[stage],
            sum_recv.at[landing, frame, stage],
            me + (1 - 2 * own_bits[stage]) * (1 << stage),
        )

    def side_rows(phase):
        row_side = far_side if phase else side
        return pl.ds(pl.multiple_of(row_side * low, LANES), low)

    def collect(stage, phase, frame):
        last = stage == bits - 1
        sum_copy(stage, 1 - phase if last else phase, frame).wait_recv()
        total = kept_part(stage, phase, frame, False)[...] + gots[stage][phase, frame]
        if last:
            total_ref[frame, :, side_rows(phase)] = total
        else:
            sums[stage + 1][phase, frame] = total

    pl.semaphore_wait(pltpu.get_barrier_semaphore(), len(peers))
    early = near // 2
    for hop in near_hops + far_hops[:early]:
        for coil in range(coils):
            maps_copy(hop, coil).start()
    drain(sens_v, load_sem.at[0])
    drain(image_v, load_sem.at[1])
    pack_kernel(devices, width, sens_v, image_v, packed_ref)
    for at in range(near - 1):
        if at < early:
            for coil in range(coils):
                maps_copy(far_hops[early + at], coil).start()
        pack_copy(near_hops[at]).start()
    for hop in far_hops:
        if hop // 2 % 2 == 0:
            pack_copy(hop).start()
    for coil in range(coils):
        maps_ref[coil, own_rows, :] = sens_v[me * coils + coil]
    landed_ref[me] = packed_ref[me]

    lane = lax.broadcasted_iota(jnp.int32, (length, 2 * length), 1)
    line = lax.broadcasted_iota(jnp.int32, (length, 2 * length), 0)
    picked = line == 2 * (lane % low) + lane // length
    mask_v[...] = dot(
        mask_ref[...].astype(jnp.float32).astype(jnp.bfloat16),
        jnp.where(picked, 1.0, 0.0).astype(jnp.bfloat16),
    )
    drain(rows_v, load_sem.at[2])
    drain(cols_v, load_sem.at[3])
    drain(data_ref, load_sem.at[4])

    def transform(frame):
        mixes = []
        for odd in range(2):
            weight = mask_v[pl.ds(frame, 1), odd * length : (odd + 1) * length].astype(jnp.bfloat16)
            top, rest_part = (rows_v[odd, 0] * weight, rows_v[odd, 1] * weight)
            mixes.append(jnp.concatenate([rest_part, top, top], 1))
            right = jnp.concatenate([rows_v[odd, 0], rows_v[odd, 1], rows_v[odd, 0]], 1)
            gram = lax.dot_general(
                mixes[-1], right, (((1,), (1,)), ((), ())), preferred_element_type=jnp.float32
            )
            top, rest_part = split(gram)
            gram_ref[frame, odd, 0] = top
            gram_ref[frame, odd, 1] = rest_part
        for coil in range(coils):
            parts = []
            for odd in range(2):
                lines = data_ref[coil * frames + frame, odd]
                lines = jnp.concatenate([lines[:, :half], lines[:, half:]], 0)
                parts.append(dot(mixes[odd], mix_right(split(lines))))
            near, far = (parts[0] + parts[1], parts[0] - parts[1])
            mid = jnp.concatenate(
                [
                    jnp.concatenate([near[:low], near[low:]], 1),
                    jnp.concatenate([far[:low], far[low:]], 1),
                ],
                0,
            )
            base_ref[coil, frame] = dot(mix_left(mid), mix_right(cols_v))

    def weigh(phase, frame):
        real, imag = (0.0, 0.0)
        lines = side_rows(phase)
        for coil in range(coils):
            base_re, base_im = (
                base_ref[coil, frame, lines, :half],
                base_ref[coil, frame, lines, half:],
            )
            maps_re, maps_im = (maps_ref[coil, lines, :half], maps_ref[coil, lines, half:])
            real = real + maps_re * base_re + maps_im * base_im
            imag = imag + maps_re * base_im - maps_im * base_re
        shape = (2,) * bits + (width, low)
        lead = (phase, frame) + (slice(None),) * bits
        sums[0][lead + (slice(0, width),)] = jnp.transpose(real).reshape(shape)
        sums[0][lead + (slice(width, 2 * width),)] = jnp.transpose(imag).reshape(shape)

    def pass_on(stage, phase, frame):
        if 0 <= frame < frames:
            collect(stage, phase, frame)
            sum_copy(stage + 1, phase, frame).start()

    def offer(phase, frame):
        if frame < frames:
            weigh(phase, frame)
            sum_copy(0, phase, frame).start()
        pass_on(0, phase, frame - 1)

    lead = min(1, frames - 1)

    def step(frame, unused):
        transform(frame)

        @pl.when(frame == lead)
        def wait_near():
            drain(maps_ref.at[:, pl.ds(0, (near - 1) * rows), :], maps_recv.at[0])

        @pl.when(frame >= lead)
        def offer_near():
            weigh(0, frame - lead)
            sum_copy(0, 0, frame - lead).start()

        @pl.when(frame > lead)
        def pass_near():
            collect(0, 0, frame - lead - 1)
            sum_copy(1, 0, frame - lead - 1).start()

        return unused

    lax.fori_loop(0, frames, step, 0)
    for turn in range(frames - lead, frames + 1):
        offer(0, turn)
    for hop in far_hops:
        if hop // 2 % 2:
            pack_copy(hop).start()
    drain(maps_ref.at[:, pl.ds(0, near * rows), :], maps_recv.at[1])

    def project(sweep, frame):
        shape = (all_coils, width, length)
        maps_re, maps_im = (own_ref[:, 0].reshape(shape), own_ref[:, 1].reshape(shape))
        now_re, now_im = (now_ref[sweep, 0, frame][None], now_ref[sweep, 1, frame][None])
        seen_re = (maps_re * now_re - maps_im * now_im).reshape(all_coils * width, length)
        seen_im = (maps_re * now_im + maps_im * now_re).reshape(all_coils * width, length)
        parts = []
        for odd in range(2):
            if odd:
                both = [part[:, :low] - part[:, low:] for part in (seen_re, seen_im)]
            else:
                both = [part[:, :low] + part[:, low:] for part in (seen_re, seen_im)]
            parts.append(dot(mix_left(jnp.concatenate(both, 1)), mix_right(gram_ref[frame, odd])))
        near, far = (parts[0] + parts[1], parts[0] - parts[1])
        kept_re = jnp.concatenate([near[:, :low], far[:, :low]], 1).reshape(shape)
        kept_im = jnp.concatenate([near[:, low:], far[:, low:]], 1).reshape(shape)
        grad_ref[sweep, 0, frame] = jnp.sum(maps_re * kept_re + maps_im * kept_im, 0)
        grad_ref[sweep, 1, frame] = jnp.sum(maps_re * kept_im - maps_im * kept_re, 0)

    def turn_maps():
        lines = pl.ds(pl.multiple_of(far_side * low, LANES), low)
        for coil in range(coils):
            for part in range(2):
                lanes = pl.ds(pl.multiple_of(part * half + side * (half // 2), LANES), half // 2)
                turned = jnp.transpose(maps_ref[coil, lines, lanes])
                relay_ref[:, part, coil] = turned.reshape(near, width, low)
        for hop in near_hops:
            relay_copy(hop).start()
        relay_part(side, me % near * coils, far_side)[...] = relay_ref[me % near]

    def unfold(target, row_side, lines, lanes):
        turned = jnp.transpose(landed_ref[lines, :, lanes].reshape(low, -1))
        rows_at = pl.ds(pl.multiple_of(row_side * low, LANES), low)
        target[..., rows_at] = turned.reshape(target.shape[:-1] + (low,))

    def take_columns():
        drain(landed_ref.at[pl.ds(0, near - 1)], pack_recv.at[0])
        drain(landed_ref.at[pl.ds(0, near), :, pl.ds(0, block + held_lanes)], pack_recv.at[1])
        drain(relay_ref.at[pl.ds(0, near - 1)], relay_recv.at[0])
        for row_side in (side, far_side):
            lines = pl.ds(row_side * near, near)
            unfold(now_ref.at[0], row_side, lines, pl.ds(block, held_lanes))
        for coil_side, row_side in ((0, side), (1, side), (far_side, far_side)):
            start = pl.multiple_of(coil_side * (block + held_lanes), LANES)
            lines = pl.ds(row_side * near, near)
            unfold(own_ref.at[coil_side], row_side, lines, pl.ds(start, block))

    for turn in range(frames + 1):
        offer(1, turn)
        if turn == 0:
            turn_maps()
        pass_on(1, 0, turn)
    projected = [0] * OUTER
    summed = [0]
    known = {}

    def project_to(sweep, count):
        while projected[sweep] < min(count, frames):
            frame = projected[sweep]
            if sweep:
                for part in range(2):
                    now_ref[sweep, part, frame] = primal(sweep - 1, part, INNER, frame)
            if sweep:
                prepare(sweep - 1, frame + INNER)
            project(sweep, frame)
            projected[sweep] += 1
            if sweep == OUTER - 1:
                prepare(sweep, frame)

    def target_of(sweep, part, frame):
        project_to(sweep, frame + 1)
        while summed[0] <= frame:
            for phase in range(2):
                collect(bits - 1, phase, summed[0])
            summed[0] += 1
        data_term = total_ref[frame, part * width : (part + 1) * width]
        gradient = grad_ref[sweep, part, frame] - data_term
        return now_ref[sweep, part, frame] - step_size * gradient

    def dual_time(sweep, part, count, frame):
        ahead = primal(sweep, part, count - 1, frame + 1)
        steps = dual_step * (ahead - primal(sweep, part, count - 1, frame))
        if count > 1:
            steps = recall(dual_time, sweep, part, count - 1, frame) + steps
        return clipped(steps)

    def dual_rows(sweep, part, count, frame):
        steps = dual_step * row_steps(primal(sweep, part, count - 1, frame))
        if count > 1:
            steps = recall(dual_rows, sweep, part, count - 1, frame) + steps
        return clipped(steps)

    def rows_apart(sweep, part, count, frame):
        return spread_rows(recall(dual_rows, sweep, part, count, frame))

    def prepare(sweep, newest):
        for count in range(1, INNER + 1):
            if 0 <= newest - count + 1 < frames:
                for part in range(2):
                    recall(rows_apart, sweep, part, count, newest - count + 1)

    def lowered(sweep, part, count, frame):
        moved = recall(rows_apart, sweep, part, count, frame)
        if frame > 0:
            moved = moved + recall(dual_time, sweep, part, count, frame - 1)
        if frame < frames - 1:
            moved = moved - recall(dual_time, sweep, part, count, frame)
        return recall(target_of, sweep, part, frame) - tv_weight * moved

    def recall(rule, *where):
        if (rule, where) not in known:
            known[rule, where] = rule(*where)
        return known[rule, where]

    def primal(sweep, part, count, frame):
        if count:
            return recall(lowered, sweep, part, count, frame)
        return recall(target_of, sweep, part, frame)

    def back_copy(piece, hop):
        peer = peers[hop - 1]
        return remote(
            ready_ref.at[piece, peer],
            back_ref.at[piece, me],
            back_send.at[piece],
            back_recv.at[piece],
            peer,
        )

    for turn in range(frames):
        pass_on(1, 1, turn)
        pass_on(2, 0, turn)
        pass_on(2, 1, turn - 2)
        if turn == 1:
            take_columns()
        if turn:
            project_to(0, (turn * frames + 2) // 5)

    for frame in range(frames - 2, frames):
        if bits == 4:
            project_to(1, frame + 3 - frames)
        pass_on(2, 1, frame)
    for stage in range(3, bits - 1):
        for phase in range(2):
            for frame in range(frames):
                pass_on(stage, phase, frame)

    for piece in range(2):
        settled = []
        for frame in range(piece * some, (piece + 1) * some):
            settled.append([primal(OUTER - 1, part, INNER, frame) for part in range(2)])
        settled = [pair[0] for pair in settled] + [pair[1] for pair in settled]
        turned = jnp.transpose(jnp.concatenate(settled, 0))
        ready_ref[piece] = turned.reshape(ready_ref.shape[1:])
        for hop in far_hops[::-1] + near_hops[::-1]:
            back_copy(piece, hop).start()
        back_ref[piece, me] = ready_ref[piece, me]
    for piece in range(2):
        drain(back_ref.at[piece, pl.ds(0, devices - 1)], back_recv.at[piece])
        for first in range(0, frames, group):
            for tile in range(devices // group):
                taken = [
                    back_ref[piece, tile * group + at, :, first * width : first * width + LANES]
                    for at in range(group)
                ]
                for at, value in enumerate(swap_blocks(taken, width)):
                    part, frame = ((first + at) // some, piece * some + (first + at) % some)
                    target = part * half + tile * LANES
                    out_ref[:, frame, target : target + LANES] = value
    drain(maps_ref.at[:, pl.ds(0, (devices - 1) * rows), :], maps_send.at[0])
    drain(landed_ref.at[pl.ds(0, near - 1)], pack_send.at[0])
    drain(landed_ref.at[pl.ds(0, near), :, pl.ds(0, block + held_lanes)], pack_send.at[1])
    drain(relay_ref.at[pl.ds(0, near - 1)], relay_send.at[0])
    for piece in range(2):
        drain(back_ref.at[piece, pl.ds(0, devices - 1)], back_send.at[piece])
    for stage in range(bits):
        drain(gots[stage], sum_send.at[stage])


def reconstruct(image, sens, kspace, mask, devices):
    rows, frames, packed = image.shape
    all_coils = sens.shape[1]
    length, pairs, unused = kspace.shape
    coils = pairs // frames
    bits = devices.bit_length() - 1
    width = packed // 2 // devices
    lanes = 2 * (all_coils + frames) * width
    row_pairs = row_tables(length)
    col_pair = column_table(packed // 2)
    whole = pl.BlockSpec(memory_space=pltpu.VMEM)
    apart = pl.BlockSpec(memory_space=pl.ANY)

    def held(*shape):
        return pltpu.VMEM(shape, jnp.float32)

    dma = pltpu.SemaphoreType.DMA
    block = (2 * width, length // 2)
    sums = [held(2, frames, *(2,) * (bits - stage), *block) for stage in range(bits)]
    gots = [held(2, frames, *(2,) * (bits - 1 - stage), *block) for stage in range(bits)]
    return pl.pallas_call(
        lambda *refs: whole_kernel(devices, *refs),
        out_shape=jax.ShapeDtypeStruct((rows, frames, packed), jnp.float32),
        in_specs=[apart] * 3 + [whole] + [apart] * 2,
        out_specs=whole,
        scratch_shapes=[
            held(all_coils, rows, packed),
            held(frames, rows, packed),
            pltpu.VMEM(row_pairs.shape, jnp.bfloat16),
            pltpu.VMEM(col_pair.shape, jnp.bfloat16),
            held(pairs, 2, length // 2, packed),
            held(frames, 2 * length),
            held(coils, frames, length, packed),
            held(coils, length, packed),
            held(devices, rows, lanes),
            held(devices, rows, lanes),
            held(2, 2, all_coils // 2, width, length),
            held(OUTER, 2, frames, width, length),
            held(OUTER, 2, frames, width, length),
            pltpu.VMEM((frames, 2, 2, length, length), jnp.bfloat16),
            held(devices // 2, 2, coils, width, length // 2),
            held(frames, 2 * width, length),
            held(2, devices, rows, frames * width),
            held(2, devices, rows, frames * width),
            *sums,
            *gots,
            dma((5,)),
            dma((1,)),
            dma((2,)),
            dma((2,)),
            dma((2,)),
            dma((1,)),
            dma((1,)),
            dma((bits,)),
            dma((2, frames, bits)),
            dma((2,)),
            dma((2,)),
        ],
        compiler_params=pltpu.CompilerParams(
            collective_id=0, has_side_effects=True, vmem_limit_bytes=60 * 1024 * 1024
        ),
        name="reconstruct",
    )(
        image,
        sens,
        kspace.reshape(length // 2, 2, pairs, packed),
        mask,
        jnp.asarray(row_pairs),
        jnp.asarray(col_pair),
    )


def per_device(image, sens, kspace, mask):
    devices = lax.axis_size("coil")
    device = lax.axis_index("coil")
    rows_dev, frames, packed = image.shape
    coils = sens.shape[1]
    length, pairs, unused = kspace.shape
    half = packed // 2
    width = half // devices
    copies = max(1, frames // pairs)
    own_coils = max(1, pairs // frames)
    own_frames = min(frames, pairs)
    if blocked(devices, width, rows_dev, length, half, coils, frames, pairs):
        return reconstruct(image, sens, kspace, mask, devices)
    row_cos, row_sin = dft_tables(length)
    col_cos, col_sin = dft_tables(half)
    mask_float = mask.astype(jnp.float32)
    real, imag = projections(mask, row_cos, row_sin)
    spread = sens if copies == 1 else jnp.repeat(sens, copies, axis=1)
    own_maps = lax.all_to_all(spread, "coil", split_axis=1, concat_axis=0, tiled=True)
    outgoing = jnp.concatenate([to_columns(sens, devices), to_columns(image, devices)], 2)
    incoming = lax.all_to_all(outgoing, "coil", split_axis=0, concat_axis=0, tiled=True)
    columns = jnp.transpose(incoming.reshape(length, -1))
    first_frame = device * pairs % frames
    local_mask = lax.dynamic_slice_in_dim(mask_float, first_frame, own_frames, 0)
    mask_pairs = jnp.tile(local_mask, (own_coils, 1))
    base_re, base_im = data_images(kspace, mask_pairs, row_cos, row_sin, col_cos, col_sin)
    base_re = base_re.reshape(length, own_coils, own_frames, half)
    base_im = base_im.reshape(length, own_coils, own_frames, half)
    own_re, own_im = (own_maps[:, :, None, :half], own_maps[:, :, None, half:])
    term_re = jnp.sum(own_re * base_re + own_im * base_im, 1)
    term_im = jnp.sum(own_re * base_im - own_im * base_re, 1)
    term = jnp.transpose(jnp.stack([term_re, term_im]), (3, 0, 2, 1))
    if own_frames < frames:
        wide = jnp.zeros((half, 2, frames, length), jnp.float32)
        term = lax.dynamic_update_slice_in_dim(wide, term, first_frame, 2)
    term = term.reshape(devices, width, 2, frames, length)
    data_term = lax.psum_scatter(term, "coil", scatter_dimension=0, tiled=True)
    data_term = jnp.transpose(data_term[0], (1, 2, 0, 3))

    cut = 2 * coils * width
    maps = columns[:cut].reshape(2, coils, width, length)
    field = columns[cut:].reshape(2, frames, width, length)
    field = iterate(field, data_term, maps, real, imag)

    leaving = jnp.transpose(field.reshape(2 * frames * width, length))
    leaving = leaving.reshape(devices, rows_dev, 2 * frames * width)
    arrived = lax.all_to_all(leaving, "coil", split_axis=0, concat_axis=0, tiled=True)
    arrived = arrived.reshape(devices, rows_dev, 2, frames, width)
    return jnp.transpose(arrived, (1, 3, 2, 0, 4)).reshape(rows_dev, frames, packed)


def solution(mesh):
    return jax.shard_map(
        per_device,
        mesh=mesh,
        in_specs=(
            P(("plane", "coil"), None, None),
            P(("plane", "coil"), None, None),
            P("plane", "coil", None),
            P(),
        ),
        out_specs=P(("plane", "coil"), None, None),
        check_vma=False,
    )
```

```python
import jax
import jax.numpy as jnp
import numpy as np
from jax import lax
from jax.experimental import pallas as pl
from jax.experimental.pallas import tpu as pltpu
from jax.sharding import PartitionSpec as P

OUTER = 2
INNER = 2

step_size = 0.5
tv_weight = 0.1
dual_step = 1.25
high = lax.Precision.HIGH


def contract(spec, *operands):
    return jnp.einsum(spec, *operands, precision=high, preferred_element_type=jnp.float32)


def dft_tables(length):
    index = lax.iota(jnp.int32, length)
    product = index[:, None] * index[None, :] % length
    angle = 2.0 * jnp.pi / length * product.astype(jnp.float32)
    scale = 1.0 / jnp.sqrt(jnp.float32(length))
    return (jnp.cos(angle) * scale, -jnp.sin(angle) * scale)


def column_matrix(cos_part, sin_part):
    upper = jnp.concatenate([cos_part, sin_part], 1)
    lower = jnp.concatenate([-sin_part, cos_part], 1)
    return jnp.concatenate([upper, lower], 0)


def projections(mask, row_cos, row_sin):
    weights = mask.astype(jnp.float32)
    wide = jnp.concatenate([row_cos, row_sin], 1)
    cos_rows = weights[:, :, None] * row_cos[None]
    sin_rows = weights[:, :, None] * row_sin[None]
    from_cos = contract("fka,ky->fay", cos_rows, wide)
    from_sin = contract("fka,ky->fay", sin_rows, wide)
    length = row_cos.shape[0]
    real = from_cos[..., :length] + from_sin[..., length:]
    imag = from_cos[..., length:] - from_sin[..., :length]
    return (real, imag)


def to_columns(field, devices):
    rows, count, packed = field.shape
    width = packed // 2 // devices
    parts = field.reshape(rows, count, 2, devices, width)
    return jnp.transpose(parts, (3, 0, 2, 1, 4)).reshape(devices, rows, 2 * count * width)


def divergence(dual_time, dual_rows):
    time_axis, row_axis = 1, 3
    zero_time = jnp.zeros_like(dual_time[:, :1])
    zero_rows = jnp.zeros_like(dual_rows[..., :1])
    head_time = dual_time[:, :-1]
    head_rows = dual_rows[..., :-1]
    from_time = jnp.concatenate([zero_time, head_time], time_axis) - jnp.concatenate(
        [head_time, zero_time], time_axis
    )
    from_rows = jnp.concatenate([zero_rows, head_rows], row_axis) - jnp.concatenate(
        [head_rows, zero_rows], row_axis
    )
    return from_time + from_rows


def forward_diff(field):
    diff_time = jnp.concatenate(
        [field[:, 1:] - field[:, :-1], jnp.zeros_like(field[:, :1])], 1
    )
    diff_rows = jnp.concatenate(
        [field[..., 1:] - field[..., :-1], jnp.zeros_like(field[..., :1])], 3
    )
    return (diff_time, diff_rows)


def denoise(target):
    dual_time = jnp.zeros_like(target)
    dual_rows = jnp.zeros_like(target)
    for repeat in range(INNER):
        primal = target
        if repeat:
            primal = target - tv_weight * divergence(dual_time, dual_rows)
        diff_time, diff_rows = forward_diff(primal)
        dual_time = jnp.clip(dual_time + dual_step * diff_time, -1.0, 1.0)
        dual_rows = jnp.clip(dual_rows + dual_step * diff_rows, -1.0, 1.0)
    return target - tv_weight * divergence(dual_time, dual_rows)


def iterate(field, data_term, maps, real, imag):
    maps_re, maps_im = (maps[0][None], maps[1][None])
    for sweep in range(OUTER):
        now_re, now_im = (field[0][:, None], field[1][:, None])
        seen_re = maps_re * now_re - maps_im * now_im
        seen_im = maps_re * now_im + maps_im * now_re
        kept_re = contract("fczy,fky->fczk", seen_re, real) - contract(
            "fczy,fky->fczk", seen_im, imag
        )
        kept_im = contract("fczy,fky->fczk", seen_re, imag) + contract(
            "fczy,fky->fczk", seen_im, real
        )
        grad_re = jnp.sum(maps_re * kept_re + maps_im * kept_im, 1)
        grad_im = jnp.sum(maps_re * kept_im - maps_im * kept_re, 1)
        gradient = jnp.stack([grad_re, grad_im]) - data_term
        field = denoise(field - step_size * gradient)
    return field


def data_images(kspace, mask_pairs, row_cos, row_sin, col_cos, col_sin):
    masked = jnp.transpose(mask_pairs)[:, :, None] * kspace
    mid = contract("kpz,zw->kpw", masked, column_matrix(col_cos, -col_sin))
    half = kspace.shape[-1] // 2
    from_cos = contract("ky,kpz->ypz", row_cos, mid)
    from_sin = contract("ky,kpz->ypz", row_sin, mid)
    real = from_cos[..., :half] + from_sin[..., half:]
    imag = from_cos[..., half:] - from_sin[..., :half]
    return (real, imag)


LANES = 128
SUBLANES = 8


def swap_blocks(values, width):
    count = len(values)
    block = lax.broadcasted_iota(jnp.int32, values[0].shape, 1) // width
    step = count // 2
    while step:
        lower = block // step % 2 == 0
        shift = step * width
        values = list(values)
        for at in range(count):
            if at // step % 2 == 0:
                near, far = (values[at], values[at + step])
                values[at] = jnp.where(lower, near, pltpu.roll(far, shift, 1))
                values[at + step] = jnp.where(lower, pltpu.roll(near, LANES - shift, 1), far)
        step //= 2
    return values


def blocked(devices, width, rows, length, half, coils, frames, pairs):
    group = LANES // width
    fits = LANES % width == 0 and width % SUBLANES == 0 and rows % SUBLANES == 0
    fits = fits and devices % group == 0 and coils % (2 * group) == 0 and frames % group == 0
    fits = fits and devices & (devices - 1) == 0
    fits = fits and devices >= 16 and frames % 2 == 0 and pairs % frames == 0 and coils * frames == pairs * devices
    return fits and length % (2 * LANES) == 0 and half % (2 * LANES) == 0


def pack_kernel(devices, width, sens_ref, image_ref, out_ref):
    group = LANES // width
    half = devices * width
    near = sens_ref.shape[0] // 2
    start = 0
    for source, origin, count in (
        (sens_ref, 0, near),
        (image_ref, 0, image_ref.shape[0]),
        (sens_ref, near, near),
    ):
        for part in range(2):
            for tile in range(half // LANES):
                lane = part * half + tile * LANES
                for first in range(0, count, group):
                    taken = [
                        source[origin + first + at, :, lane : lane + LANES] for at in range(group)
                    ]
                    target = start + (part * count + first) * width
                    for at, value in enumerate(swap_blocks(taken, width)):
                        out_ref[tile * group + at, :, target : target + LANES] = value
        start += 2 * count * width


def split(value):
    top = value.astype(jnp.bfloat16)
    return (top, (value - top.astype(jnp.float32)).astype(jnp.bfloat16))


def narrow(value):
    value = value.astype(np.float32)
    top = value.astype(jnp.bfloat16)
    return np.stack([top, (value - top.astype(np.float32)).astype(jnp.bfloat16)])


def mix_left(value):
    top, low = split(value)
    return jnp.concatenate([low, top, top], 1)


def mix_right(pair):
    return jnp.concatenate([pair[0], pair[1], pair[0]], 0)


def dot(left, right):
    return jnp.dot(left, right, preferred_element_type=jnp.float32)


def row_tables(length):
    half = length // 2
    tables = []
    for odd in range(2):
        product = np.outer(np.arange(half), 2 * np.arange(half) + odd) % length
        angle = 2.0 * np.pi / length * product
        cos_part, sin_part = (np.cos(angle) / np.sqrt(length), np.sin(angle) / np.sqrt(length))
        tables.append(narrow(np.block([[cos_part, -sin_part], [sin_part, cos_part]])))
    return np.stack(tables)


def column_table(length):
    angle = 2.0 * np.pi / length * (np.outer(np.arange(length), np.arange(length)) % length)
    cos_part, sin_part = (np.cos(angle) / np.sqrt(length), np.sin(angle) / np.sqrt(length))
    return narrow(np.block([[cos_part, sin_part], [-sin_part, cos_part]]))


MESH = pl.DeviceIdType.MESH


def announce(peers):
    for peer in peers:
        pl.semaphore_signal(
            pltpu.get_barrier_semaphore(), 1, device_id={"coil": peer}, device_id_type=MESH
        )


def drain(whole, sem):
    pltpu.make_async_copy(whole, whole, sem).wait()


def shift_rows(value, step):
    length = value.shape[1]
    rolled = pltpu.roll(value, step % length, 1)
    at = lax.broadcasted_iota(jnp.int32, value.shape, 1)
    kept = at >= step if step > 0 else at < length + step
    return jnp.where(kept, rolled, 0.0)


def spread_rows(dual):
    return shift_rows(dual, 1) - dual


def row_steps(primal):
    length = primal.shape[1]
    at = lax.broadcasted_iota(jnp.int32, primal.shape, 1)
    return jnp.where(at < length - 1, pltpu.roll(primal, length - 1, 1) - primal, 0.0)


def clipped(value):
    return jnp.minimum(jnp.maximum(value, -1.0), 1.0)


def whole_kernel(
    devices,
    image_ref,
    sens_ref,
    kspace_ref,
    mask_ref,
    rows_ref,
    cols_ref,
    out_ref,
    sens_v,
    image_v,
    rows_v,
    cols_v,
    data_ref,
    mask_v,
    base_ref,
    maps_ref,
    packed_ref,
    landed_ref,
    own_ref,
    now_ref,
    grad_ref,
    gram_ref,
    relay_ref,
    total_ref,
    ready_ref,
    back_ref,
    *rest,
):
    bits = devices.bit_length() - 1
    sums = rest[:bits]
    gots = rest[bits : 2 * bits]
    (
        load_sem,
        maps_send,
        maps_recv,
        pack_send,
        pack_recv,
        relay_send,
        relay_recv,
        sum_send,
        sum_recv,
        back_send,
        back_recv,
    ) = rest[2 * bits :]
    coils, frames, length, packed = base_ref.shape
    rows, all_coils, unused = sens_ref.shape
    half = packed // 2
    low = length // 2
    width = half // devices
    group = LANES // width
    me = lax.axis_index("coil")
    own_bits = [me // (1 << bit) % 2 for bit in range(bits)]
    inner = (own_bits[bits - 1] + own_bits[bits - 2]) % 2
    peers = []
    for hop in range(1, devices):
        turns = [hop >> bit for bit in range(bits)]
        if hop >= devices // 2:
            turns[bits - 2] += inner
        flips = [(own_bits[bit] + turns[bit]) % 2 * (1 << bit) for bit in range(bits)]
        peers.append(sum(flips[1:], flips[0]))
    near = devices // 2
    some = frames // 2
    side = me // near
    far_side = 1 - side
    near_hops = list(range(1, near))
    far_hops = list(range(near, devices))
    block = all_coils * width
    held_lanes = 2 * frames * width
    own_rows = pl.ds(pl.multiple_of(me * rows, SUBLANES), rows)

    announce(peers)
    for coil in range(all_coils):
        pltpu.make_async_copy(sens_ref.at[:, coil, :], sens_v.at[coil], load_sem.at[0]).start()
    for frame in range(frames):
        pltpu.make_async_copy(image_ref.at[:, frame, :], image_v.at[frame], load_sem.at[1]).start()
    pltpu.make_async_copy(rows_ref, rows_v, load_sem.at[2]).start()
    pltpu.make_async_copy(cols_ref, cols_v, load_sem.at[3]).start()
    for pair in range(coils * frames):
        for odd in range(2):
            pltpu.make_async_copy(
                kspace_ref.at[:, odd, pair, :], data_ref.at[pair, odd], load_sem.at[4]
            ).start()

    def remote(source, target, send, recv, peer):
        return pltpu.make_async_remote_copy(
            src_ref=source,
            dst_ref=target,
            send_sem=send,
            recv_sem=recv,
            device_id={"coil": peer},
            device_id_type=MESH,
        )

    def maps_copy(hop, coil):
        peer = peers[hop - 1]
        return remote(
            sens_ref.at[:, peer * coils + coil, :],
            maps_ref.at[coil, own_rows, :],
            maps_send.at[0],
            maps_recv.at[hop // near],
            peer,
        )

    def pack_copy(hop):
        peer = peers[hop - 1]
        if hop < near:
            lanes = pl.ds(0, 2 * block + held_lanes)
        else:
            lanes = pl.ds(pl.multiple_of(side * block, LANES), block + held_lanes)
        return remote(
            packed_ref.at[peer, :, lanes],
            landed_ref.at[me, :, lanes],
            pack_send.at[hop // near],
            pack_recv.at[hop // near],
            peer,
        )

    def relay_part(coil_side, first, row_side):
        lanes = pl.ds(pl.multiple_of(row_side * low, LANES), low)
        return own_ref.at[coil_side, :, pl.ds(first, coils), :, lanes]

    def relay_copy(hop):
        peer = peers[hop - 1]
        return remote(
            relay_ref.at[peer % near],
            relay_part(side, me % near * coils, far_side),
            relay_send.at[0],
            relay_recv.at[0],
            peer,
        )

    def kept_part(stage, phase, frame, other):
        at = own_bits[stage]
        at = 1 - at if other else at
        lead = (slice(None),) * (bits - 1 - stage)
        return sums[stage].at[(phase, frame) + lead + (at,)]

    def sum_copy(stage, phase, frame):
        landing = 1 - phase if stage == bits - 1 else phase
        return remote(
            kept_part(stage, phase, frame, True),
            gots[stage].at[landing, frame],
            sum_send.at[stage],
            sum_recv.at[landing, frame, stage],
            me + (1 - 2 * own_bits[stage]) * (1 << stage),
        )

    def side_rows(phase):
        row_side = far_side if phase else side
        return pl.ds(pl.multiple_of(row_side * low, LANES), low)

    def collect(stage, phase, frame):
        last = stage == bits - 1
        sum_copy(stage, 1 - phase if last else phase, frame).wait_recv()
        total = kept_part(stage, phase, frame, False)[...] + gots[stage][phase, frame]
        if last:
            total_ref[frame, :, side_rows(phase)] = total
        else:
            sums[stage + 1][phase, frame] = total

    pl.semaphore_wait(pltpu.get_barrier_semaphore(), len(peers))
    early = near // 2
    for hop in near_hops + far_hops[:early]:
        for coil in range(coils):
            maps_copy(hop, coil).start()
    drain(sens_v, load_sem.at[0])
    drain(image_v, load_sem.at[1])
    pack_kernel(devices, width, sens_v, image_v, packed_ref)
    for at in range(near - 1):
        if at < early:
            for coil in range(coils):
                maps_copy(far_hops[early + at], coil).start()
        pack_copy(near_hops[at]).start()
    for hop in far_hops:
        if hop // 2 % 2 == 0:
            pack_copy(hop).start()
    for coil in range(coils):
        maps_ref[coil, own_rows, :] = sens_v[me * coils + coil]
    landed_ref[me] = packed_ref[me]

    lane = lax.broadcasted_iota(jnp.int32, (length, 2 * length), 1)
    line = lax.broadcasted_iota(jnp.int32, (length, 2 * length), 0)
    picked = line == 2 * (lane % low) + lane // length
    mask_v[...] = dot(
        mask_ref[...].astype(jnp.float32).astype(jnp.bfloat16),
        jnp.where(picked, 1.0, 0.0).astype(jnp.bfloat16),
    )
    drain(rows_v, load_sem.at[2])
    drain(cols_v, load_sem.at[3])
    drain(data_ref, load_sem.at[4])

    def transform(frame):
        mixes = []
        for odd in range(2):
            weight = mask_v[pl.ds(frame, 1), odd * length : (odd + 1) * length].astype(jnp.bfloat16)
            top, rest_part = (rows_v[odd, 0] * weight, rows_v[odd, 1] * weight)
            mixes.append(jnp.concatenate([rest_part, top, top], 1))
            right = jnp.concatenate([rows_v[odd, 0], rows_v[odd, 1], rows_v[odd, 0]], 1)
            gram = lax.dot_general(
                mixes[-1], right, (((1,), (1,)), ((), ())), preferred_element_type=jnp.float32
            )
            top, rest_part = split(gram)
            gram_ref[frame, odd, 0] = top
            gram_ref[frame, odd, 1] = rest_part
        for coil in range(coils):
            parts = []
            for odd in range(2):
                lines = data_ref[coil * frames + frame, odd]
                lines = jnp.concatenate([lines[:, :half], lines[:, half:]], 0)
                parts.append(dot(mixes[odd], mix_right(split(lines))))
            near, far = (parts[0] + parts[1], parts[0] - parts[1])
            mid = jnp.concatenate(
                [
                    jnp.concatenate([near[:low], near[low:]], 1),
                    jnp.concatenate([far[:low], far[low:]], 1),
                ],
                0,
            )
            base_ref[coil, frame] = dot(mix_left(mid), mix_right(cols_v))

    def weigh(phase, frame):
        real, imag = (0.0, 0.0)
        lines = side_rows(phase)
        for coil in range(coils):
            base_re, base_im = (
                base_ref[coil, frame, lines, :half],
                base_ref[coil, frame, lines, half:],
            )
            maps_re, maps_im = (maps_ref[coil, lines, :half], maps_ref[coil, lines, half:])
            real = real + maps_re * base_re + maps_im * base_im
            imag = imag + maps_re * base_im - maps_im * base_re
        shape = (2,) * bits + (width, low)
        lead = (phase, frame) + (slice(None),) * bits
        sums[0][lead + (slice(0, width),)] = jnp.transpose(real).reshape(shape)
        sums[0][lead + (slice(width, 2 * width),)] = jnp.transpose(imag).reshape(shape)

    def pass_on(stage, phase, frame):
        if 0 <= frame < frames:
            collect(stage, phase, frame)
            sum_copy(stage + 1, phase, frame).start()

    def offer(phase, frame):
        if frame < frames:
            weigh(phase, frame)
            sum_copy(0, phase, frame).start()
        pass_on(0, phase, frame - 1)

    lead = min(1, frames - 1)

    def step(frame, unused):
        transform(frame)

        @pl.when(frame == lead)
        def wait_near():
            drain(maps_ref.at[:, pl.ds(0, (near - 1) * rows), :], maps_recv.at[0])

        @pl.when(frame >= lead)
        def offer_near():
            weigh(0, frame - lead)
            sum_copy(0, 0, frame - lead).start()

        @pl.when(frame > lead)
        def pass_near():
            collect(0, 0, frame - lead - 1)
            sum_copy(1, 0, frame - lead - 1).start()

        return unused

    lax.fori_loop(0, frames, step, 0)
    for turn in range(frames - lead, frames + 1):
        offer(0, turn)
    for hop in far_hops:
        if hop // 2 % 2:
            pack_copy(hop).start()
    drain(maps_ref.at[:, pl.ds(0, near * rows), :], maps_recv.at[1])

    def project(sweep, frame):
        shape = (all_coils, width, length)
        maps_re, maps_im = (own_ref[:, 0].reshape(shape), own_ref[:, 1].reshape(shape))
        now_re, now_im = (now_ref[sweep, 0, frame][None], now_ref[sweep, 1, frame][None])
        seen_re = (maps_re * now_re - maps_im * now_im).reshape(all_coils * width, length)
        seen_im = (maps_re * now_im + maps_im * now_re).reshape(all_coils * width, length)
        parts = []
        for odd in range(2):
            if odd:
                both = [part[:, :low] - part[:, low:] for part in (seen_re, seen_im)]
            else:
                both = [part[:, :low] + part[:, low:] for part in (seen_re, seen_im)]
            parts.append(dot(mix_left(jnp.concatenate(both, 1)), mix_right(gram_ref[frame, odd])))
        near, far = (parts[0] + parts[1], parts[0] - parts[1])
        kept_re = jnp.concatenate([near[:, :low], far[:, :low]], 1).reshape(shape)
        kept_im = jnp.concatenate([near[:, low:], far[:, low:]], 1).reshape(shape)
        grad_ref[sweep, 0, frame] = jnp.sum(maps_re * kept_re + maps_im * kept_im, 0)
        grad_ref[sweep, 1, frame] = jnp.sum(maps_re * kept_im - maps_im * kept_re, 0)

    def turn_maps():
        lines = pl.ds(pl.multiple_of(far_side * low, LANES), low)
        for coil in range(coils):
            for part in range(2):
                lanes = pl.ds(pl.multiple_of(part * half + side * (half // 2), LANES), half // 2)
                turned = jnp.transpose(maps_ref[coil, lines, lanes])
                relay_ref[:, part, coil] = turned.reshape(near, width, low)
        for hop in near_hops:
            relay_copy(hop).start()
        relay_part(side, me % near * coils, far_side)[...] = relay_ref[me % near]

    def unfold(target, row_side, lines, lanes):
        turned = jnp.transpose(landed_ref[lines, :, lanes].reshape(low, -1))
        rows_at = pl.ds(pl.multiple_of(row_side * low, LANES), low)
        target[..., rows_at] = turned.reshape(target.shape[:-1] + (low,))

    def take_columns():
        drain(landed_ref.at[pl.ds(0, near - 1)], pack_recv.at[0])
        drain(landed_ref.at[pl.ds(0, near), :, pl.ds(0, block + held_lanes)], pack_recv.at[1])
        drain(relay_ref.at[pl.ds(0, near - 1)], relay_recv.at[0])
        for row_side in (side, far_side):
            lines = pl.ds(row_side * near, near)
            unfold(now_ref.at[0], row_side, lines, pl.ds(block, held_lanes))
        for coil_side, row_side in ((0, side), (1, side), (far_side, far_side)):
            start = pl.multiple_of(coil_side * (block + held_lanes), LANES)
            lines = pl.ds(row_side * near, near)
            unfold(own_ref.at[coil_side], row_side, lines, pl.ds(start, block))

    for turn in range(frames + 1):
        if turn == 0:
            turn_maps()
        offer(1, turn)
        pass_on(1, 0, turn)
    projected = [0] * OUTER
    summed = [0]
    known = {}

    def project_to(sweep, count):
        while projected[sweep] < min(count, frames):
            frame = projected[sweep]
            if sweep:
                for part in range(2):
                    now_ref[sweep, part, frame] = primal(sweep - 1, part, INNER, frame)
            if sweep:
                prepare(sweep - 1, frame + INNER)
            project(sweep, frame)
            projected[sweep] += 1
            if sweep == OUTER - 1:
                prepare(sweep, frame)

    def target_of(sweep, part, frame):
        project_to(sweep, frame + 1)
        while summed[0] <= frame:
            for phase in range(2):
                collect(bits - 1, phase, summed[0])
            summed[0] += 1
        data_term = total_ref[frame, part * width : (part + 1) * width]
        gradient = grad_ref[sweep, part, frame] - data_term
        return now_ref[sweep, part, frame] - step_size * gradient

    def dual_time(sweep, part, count, frame):
        ahead = primal(sweep, part, count - 1, frame + 1)
        steps = dual_step * (ahead - primal(sweep, part, count - 1, frame))
        if count > 1:
            steps = recall(dual_time, sweep, part, count - 1, frame) + steps
        return clipped(steps)

    def dual_rows(sweep, part, count, frame):
        steps = dual_step * row_steps(primal(sweep, part, count - 1, frame))
        if count > 1:
            steps = recall(dual_rows, sweep, part, count - 1, frame) + steps
        return clipped(steps)

    def rows_apart(sweep, part, count, frame):
        return spread_rows(recall(dual_rows, sweep, part, count, frame))

    def prepare(sweep, newest):
        for count in range(1, INNER + 1):
            if 0 <= newest - count + 1 < frames:
                for part in range(2):
                    recall(rows_apart, sweep, part, count, newest - count + 1)

    def lowered(sweep, part, count, frame):
        moved = recall(rows_apart, sweep, part, count, frame)
        if frame > 0:
            moved = moved + recall(dual_time, sweep, part, count, frame - 1)
        if frame < frames - 1:
            moved = moved - recall(dual_time, sweep, part, count, frame)
        return recall(target_of, sweep, part, frame) - tv_weight * moved

    def recall(rule, *where):
        if (rule, where) not in known:
            known[rule, where] = rule(*where)
        return known[rule, where]

    def primal(sweep, part, count, frame):
        if count:
            return recall(lowered, sweep, part, count, frame)
        return recall(target_of, sweep, part, frame)

    def back_copy(piece, hop):
        peer = peers[hop - 1]
        return remote(
            ready_ref.at[piece, peer],
            back_ref.at[piece, me],
            back_send.at[piece],
            back_recv.at[piece],
            peer,
        )

    for turn in range(frames):
        pass_on(1, 1, turn)
        pass_on(2, 0, turn)
        if bits == 4 and turn == frames - 1:
            project_to(1, 1)
        pass_on(2, 1, turn - 2)
        if turn == 1:
            take_columns()
        if turn:
            project_to(0, (turn * frames + 2) // 5)

    for frame in range(frames - 2, frames):
        if bits == 4:
            project_to(1, frame + 4 - frames)
        pass_on(2, 1, frame)
    for stage in range(3, bits - 1):
        for phase in range(2):
            for frame in range(frames):
                pass_on(stage, phase, frame)

    for piece in range(2):
        settled = []
        for frame in range(piece * some, (piece + 1) * some):
            settled.append([primal(OUTER - 1, part, INNER, frame) for part in range(2)])
        settled = [pair[0] for pair in settled] + [pair[1] for pair in settled]
        turned = jnp.transpose(jnp.concatenate(settled, 0))
        ready_ref[piece] = turned.reshape(ready_ref.shape[1:])
        for hop in far_hops[::-1] + near_hops[::-1]:
            back_copy(piece, hop).start()
        back_ref[piece, me] = ready_ref[piece, me]
    for piece in range(2):
        drain(back_ref.at[piece, pl.ds(0, devices - 1)], back_recv.at[piece])
        for first in range(0, frames, group):
            for tile in range(devices // group):
                taken = [
                    back_ref[piece, tile * group + at, :, first * width : first * width + LANES]
                    for at in range(group)
                ]
                for at, value in enumerate(swap_blocks(taken, width)):
                    part, frame = ((first + at) // some, piece * some + (first + at) % some)
                    target = part * half + tile * LANES
                    out_ref[:, frame, target : target + LANES] = value
    drain(maps_ref.at[:, pl.ds(0, (devices - 1) * rows), :], maps_send.at[0])
    drain(landed_ref.at[pl.ds(0, near - 1)], pack_send.at[0])
    drain(landed_ref.at[pl.ds(0, near), :, pl.ds(0, block + held_lanes)], pack_send.at[1])
    drain(relay_ref.at[pl.ds(0, near - 1)], relay_send.at[0])
    for piece in range(2):
        drain(back_ref.at[piece, pl.ds(0, devices - 1)], back_send.at[piece])
    for stage in range(bits):
        drain(gots[stage], sum_send.at[stage])


def reconstruct(image, sens, kspace, mask, devices):
    rows, frames, packed = image.shape
    all_coils = sens.shape[1]
    length, pairs, unused = kspace.shape
    coils = pairs // frames
    bits = devices.bit_length() - 1
    width = packed // 2 // devices
    lanes = 2 * (all_coils + frames) * width
    row_pairs = row_tables(length)
    col_pair = column_table(packed // 2)
    whole = pl.BlockSpec(memory_space=pltpu.VMEM)
    apart = pl.BlockSpec(memory_space=pl.ANY)

    def held(*shape):
        return pltpu.VMEM(shape, jnp.float32)

    dma = pltpu.SemaphoreType.DMA
    block = (2 * width, length // 2)
    sums = [held(2, frames, *(2,) * (bits - stage), *block) for stage in range(bits)]
    gots = [held(2, frames, *(2,) * (bits - 1 - stage), *block) for stage in range(bits)]
    return pl.pallas_call(
        lambda *refs: whole_kernel(devices, *refs),
        out_shape=jax.ShapeDtypeStruct((rows, frames, packed), jnp.float32),
        in_specs=[apart] * 3 + [whole] + [apart] * 2,
        out_specs=whole,
        scratch_shapes=[
            held(all_coils, rows, packed),
            held(frames, rows, packed),
            pltpu.VMEM(row_pairs.shape, jnp.bfloat16),
            pltpu.VMEM(col_pair.shape, jnp.bfloat16),
            held(pairs, 2, length // 2, packed),
            held(frames, 2 * length),
            held(coils, frames, length, packed),
            held(coils, length, packed),
            held(devices, rows, lanes),
            held(devices, rows, lanes),
            held(2, 2, all_coils // 2, width, length),
            held(OUTER, 2, frames, width, length),
            held(OUTER, 2, frames, width, length),
            pltpu.VMEM((frames, 2, 2, length, length), jnp.bfloat16),
            held(devices // 2, 2, coils, width, length // 2),
            held(frames, 2 * width, length),
            held(2, devices, rows, frames * width),
            held(2, devices, rows, frames * width),
            *sums,
            *gots,
            dma((5,)),
            dma((1,)),
            dma((2,)),
            dma((2,)),
            dma((2,)),
            dma((1,)),
            dma((1,)),
            dma((bits,)),
            dma((2, frames, bits)),
            dma((2,)),
            dma((2,)),
        ],
        compiler_params=pltpu.CompilerParams(
            collective_id=0, has_side_effects=True, vmem_limit_bytes=60 * 1024 * 1024
        ),
        name="reconstruct",
    )(
        image,
        sens,
        kspace.reshape(length // 2, 2, pairs, packed),
        mask,
        jnp.asarray(row_pairs),
        jnp.asarray(col_pair),
    )


def per_device(image, sens, kspace, mask):
    devices = lax.axis_size("coil")
    device = lax.axis_index("coil")
    rows_dev, frames, packed = image.shape
    coils = sens.shape[1]
    length, pairs, unused = kspace.shape
    half = packed // 2
    width = half // devices
    copies = max(1, frames // pairs)
    own_coils = max(1, pairs // frames)
    own_frames = min(frames, pairs)
    if blocked(devices, width, rows_dev, length, half, coils, frames, pairs):
        return reconstruct(image, sens, kspace, mask, devices)
    row_cos, row_sin = dft_tables(length)
    col_cos, col_sin = dft_tables(half)
    mask_float = mask.astype(jnp.float32)
    real, imag = projections(mask, row_cos, row_sin)
    spread = sens if copies == 1 else jnp.repeat(sens, copies, axis=1)
    own_maps = lax.all_to_all(spread, "coil", split_axis=1, concat_axis=0, tiled=True)
    outgoing = jnp.concatenate([to_columns(sens, devices), to_columns(image, devices)], 2)
    incoming = lax.all_to_all(outgoing, "coil", split_axis=0, concat_axis=0, tiled=True)
    columns = jnp.transpose(incoming.reshape(length, -1))
    first_frame = device * pairs % frames
    local_mask = lax.dynamic_slice_in_dim(mask_float, first_frame, own_frames, 0)
    mask_pairs = jnp.tile(local_mask, (own_coils, 1))
    base_re, base_im = data_images(kspace, mask_pairs, row_cos, row_sin, col_cos, col_sin)
    base_re = base_re.reshape(length, own_coils, own_frames, half)
    base_im = base_im.reshape(length, own_coils, own_frames, half)
    own_re, own_im = (own_maps[:, :, None, :half], own_maps[:, :, None, half:])
    term_re = jnp.sum(own_re * base_re + own_im * base_im, 1)
    term_im = jnp.sum(own_re * base_im - own_im * base_re, 1)
    term = jnp.transpose(jnp.stack([term_re, term_im]), (3, 0, 2, 1))
    if own_frames < frames:
        wide = jnp.zeros((half, 2, frames, length), jnp.float32)
        term = lax.dynamic_update_slice_in_dim(wide, term, first_frame, 2)
    term = term.reshape(devices, width, 2, frames, length)
    data_term = lax.psum_scatter(term, "coil", scatter_dimension=0, tiled=True)
    data_term = jnp.transpose(data_term[0], (1, 2, 0, 3))

    cut = 2 * coils * width
    maps = columns[:cut].reshape(2, coils, width, length)
    field = columns[cut:].reshape(2, frames, width, length)
    field = iterate(field, data_term, maps, real, imag)

    leaving = jnp.transpose(field.reshape(2 * frames * width, length))
    leaving = leaving.reshape(devices, rows_dev, 2 * frames * width)
    arrived = lax.all_to_all(leaving, "coil", split_axis=0, concat_axis=0, tiled=True)
    arrived = arrived.reshape(devices, rows_dev, 2, frames, width)
    return jnp.transpose(arrived, (1, 3, 2, 0, 4)).reshape(rows_dev, frames, packed)


def solution(mesh):
    return jax.shard_map(
        per_device,
        mesh=mesh,
        in_specs=(
            P(("plane", "coil"), None, None),
            P(("plane", "coil"), None, None),
            P("plane", "coil", None),
            P(),
        ),
        out_specs=P(("plane", "coil"), None, None),
        check_vma=False,
    )
```
